32 devices in a mesh: gz: 8 (over z, core), pair: 4 (over y, x).
Axes of the slice: x: 2, y: 2, z: 4, core: 2. Of those that a mesh axis runs over, the one named last changes fastest.
Arguments:
- orbitals: bfloat16 [8, 64, 256, 256], P(None, 'gz'), may hold values from -6 to 6
- pair_index: int32 [4, 2], P('pair'), may hold values from 0 to 7
- pair_weight: float32 [4], P('pair'), may hold values from 0.5 to 2
Outputs:
- potential: float32 [4, 64, 256, 256], P('pair', 'gz')
- residual_norm: float32 [4], P('pair')
- energy: float32 [1], replicated
The draws below stay inside these ranges and needn't reach their ends.
Inputs may be any that keep to these rules, and one draw needn't show every extreme that they name: `pair_index`: A pair may name one orbital twice.
All inputs are finite; a program needn't handle non-finite values.
Results may differ from the reference program's by a relative error of at most 0.0003.
Values sent between devices are 32-bit elements; how exact they have to be, the bound alone decides.
No kernel may reach another device: no remote copies, remote signals or barrier semaphores. Data moves between devices by JAX's collectives and lax.ppermute only.
A program may use at most 320 MiB of HBM per device.

```python
import math
import jax
import jax.numpy as jnp
from jax import lax

NX = 256
NY = 256
NORB = 8
LEVELS = 4
NU = 2
COARSE = 8
CYCLES = 1
NZ = 64
PAIRS = 4


def plant(entries, rng, least, largest):
    shape = entries.shape
    place = [jax.random.randint(jax.random.fold_in(rng, axis), (), 0, shape[axis]) for axis in range(len(shape))]
    entries = entries.at[tuple(place)].set(least)
    longest = shape.index(max(shape))
    place[longest] = (place[longest] + 1) % shape[longest]
    return entries.at[tuple(place)].set(largest)


def levels(rng, shape, split, least, high):
    def one(axis_at, blocks):
        steps = jax.random.uniform(jax.random.fold_in(jax.random.fold_in(rng, 6), axis_at), (blocks,), jnp.float32, least / len(split), high / len(split))
        return jnp.repeat(jnp.exp(steps), shape[axis_at] // blocks).reshape((-1,) + (1,) * (len(shape) - axis_at - 1))

    level = one(*split[0])
    for cut in split[1:]:
        level = level * one(*cut)
    return level


def noise(key, shape, scale, most, split=(), dtype=jnp.bfloat16):
    gain = levels(key, shape, split, -0.22, 0.18) if split else 1.0
    entries = jax.random.normal(key, shape, jnp.float32) * scale * gain
    return jnp.minimum(jnp.maximum(entries, -most), most).astype(dtype)


def setup_inputs(seed: int = 0) -> dict:
    seeds = jax.random.split(jax.random.key(seed), 4)
    orbitals = noise(seeds[0], (NORB, NZ, NY, NX), 1.0, 6.0, ((1, 8),))
    pair_index = plant(jax.random.randint(seeds[1], (PAIRS, 2), 0, NORB), jax.random.fold_in(seeds[1], 1), 0, NORB - 1).astype(jnp.int32)
    pair_weight = jnp.clip(jnp.exp(math.log(2.0) - 1.3862944 * jax.random.uniform(seeds[2], (PAIRS,), jnp.float32) ** levels(seeds[2], (PAIRS,), ((0, 4),), -0.2, 0.2)), 0.5, 2.0)
    return {"orbitals": orbitals, "pair_index": pair_index, "pair_weight": pair_weight}


relax = 2.0 / 3.0

def laplace(field, level):
    padded = jnp.pad(field, 1)
    beside = padded[2:, 1:-1, 1:-1] + padded[:-2, 1:-1, 1:-1]
    beside = beside + padded[1:-1, 2:, 1:-1] + padded[1:-1, :-2, 1:-1]
    beside = beside + padded[1:-1, 1:-1, 2:] + padded[1:-1, 1:-1, :-2]
    return (6.0 * field - beside) * 0.25 ** level

def sweep(field, source, level):
    return field + (source - laplace(field, level)) * (relax * 4.0 ** level / 6.0)

def restrict(field):
    zsize, ysize, xsize = field.shape
    return field.reshape(zsize // 2, 2, ysize // 2, 2, xsize // 2, 2).mean(axis=(1, 3, 5))

def prolong(field):
    return jnp.repeat(jnp.repeat(jnp.repeat(field, 2, axis=0), 2, axis=1), 2, axis=2)

def vcycle(field, source, level):
    if level == LEVELS - 1:
        for _ in range(COARSE):
            field = sweep(field, source, level)
        return field
    for _ in range(NU):
        field = sweep(field, source, level)
    remain = source - laplace(field, level)
    coarse_source = restrict(remain)
    correction = vcycle(jnp.zeros_like(coarse_source), coarse_source, level + 1)
    field = field + prolong(correction)
    for _ in range(NU):
        field = sweep(field, source, level)
    return field

def reference(orbitals, pair_index, pair_weight):

    def solve_pair(pair_row):
        left_orbital = orbitals[pair_row[0]].astype(jnp.float32)
        right_orbital = orbitals[pair_row[1]].astype(jnp.float32)
        density = left_orbital * right_orbital
        field = jnp.zeros_like(density)
        for _ in range(CYCLES):
            field = vcycle(field, density, 0)
        final = density - laplace(field, 0)
        return (field, jnp.sum(final * final), jnp.sum(density * field))
    potential, squares, products = lax.map(solve_pair, pair_index)
    cell_count = NZ * NY * NX
    residual_norm = jnp.sqrt(squares / cell_count)
    energy = (-0.5 * jnp.sum(pair_weight * products) / cell_count).reshape(1)
    return (potential, residual_norm, energy)
```

```python
import functools

import jax
import jax.numpy as jnp
from jax import lax
from jax.experimental import pallas as pl
from jax.experimental.pallas import tpu as pltpu
from jax.sharding import PartitionSpec as P

LANES = 128
PAD = 8
SWEEPS = 8
ROWS = 32
THIRD = 1.0 / 3.0
NINTH = 1.0 / 9.0
F32 = jnp.float32
BF16 = jnp.bfloat16
ANY = pl.BlockSpec(memory_space=pl.ANY)
VMEM = pl.BlockSpec(memory_space=pltpu.VMEM)
SMEM = pl.BlockSpec(memory_space=pltpu.SMEM)


def scale(level):
    return 4.0**level / 9.0


def iota(shape, dim):
    return lax.broadcasted_iota(jnp.int32, shape, dim)


def split_dot(value, matrix):
    high = value.astype(BF16)
    low = (value - high.astype(F32)).astype(BF16)
    return jnp.dot(high, matrix, preferred_element_type=F32) + jnp.dot(low, matrix, preferred_element_type=F32)


def to_bf16(mask, value=1.0):
    return jnp.where(mask, value, 0.0).astype(BF16)


def neighbours(ref, z, row, rows):
    parts = ref.shape[1]
    centre = [ref[z, h, pl.ds(PAD + row, rows), :] for h in range(parts)]
    lane = iota((rows, LANES), 1)
    after = [pltpu.roll(c, 1, 1) for c in centre]
    before = [pltpu.roll(c, LANES - 1, 1) for c in centre]
    sums = []
    for h in range(parts):
        total = ref[z, h, pl.ds(PAD + row - 1, rows), :] + ref[z, h, pl.ds(PAD + row + 1, rows), :]
        total += ref[z - 1, h, pl.ds(PAD + row, rows), :] + ref[z + 1, h, pl.ds(PAD + row, rows), :]
        total += jnp.where(lane == 0, after[h - 1] if h else 0.0, after[h])
        total += jnp.where(lane == LANES - 1, before[h + 1] if h + 1 < parts else 0.0, before[h])
        sums.append(total)
    return centre, sums


def zero_pads(ref, rows):
    blank = jnp.zeros((PAD, LANES), F32)

    def plane(z, _):
        for h in range(ref.shape[1]):
            ref[z, h, pl.ds(0, PAD), :] = blank
            ref[z, h, pl.ds(PAD + rows, PAD), :] = blank
        return 0

    lax.fori_loop(0, ref.shape[0], plane, 0)


def zero_planes(ref, planes, rows):
    for z in planes:
        for h in range(ref.shape[1]):
            ref[z, h, pl.ds(PAD, rows), :] = jnp.zeros((rows, LANES), F32)


def apply_planes(dst, src, first, last, shift, rows):
    def plane(z, _):
        for row in range(0, rows, ROWS):
            centre, sums = neighbours(src, z, row, ROWS)
            for h in range(len(centre)):
                dst[z + shift, h, pl.ds(PAD + row, ROWS), :] = centre[h] * THIRD + sums[h] * NINTH
        return 0

    lax.fori_loop(first, last, plane, 0)


def restrict_pair(ref, z, rows, matrices):
    total = None
    half = rows // 2
    for h in range(ref.shape[1]):

        def at(plane, offset):
            return ref[plane, h, pl.ds(PAD + offset, half, stride=2), :]

        inner = [at(z, k) + at(z + 1, k) for k in (-1, 0, 1, 2)]
        pair = inner[1] + inner[2]
        outer = inner[0] + inner[3] + (at(z - 1, 0) + at(z - 1, 1)) + (at(z + 2, 0) + at(z + 2, 1))
        part = split_dot(pair, matrices[0][h]) + split_dot(outer, matrices[1][h])
        total = part if total is None else total + part
    return total * (NINTH / 8.0)


def restrict_matrices(width, parts, out_shift=0):
    stencil, plain = [], []
    for h in range(parts):
        row = iota((LANES, LANES), 0) + h * LANES
        column = iota((LANES, LANES), 1) - out_shift
        inside = (column >= 0) & (column < width // 2)
        own = (row >> 1) == column
        beside = (row == 2 * column - 1) | (row == 2 * column + 2)
        stencil.append(jnp.where(inside & own, 6.0, jnp.where(inside & beside, 1.0, 0.0)).astype(BF16))
        plain.append(to_bf16(inside & own))
    return stencil, plain


def fine_kernel(size, orbitals, pair_index, own_a, own_b, coarse_a, coarse_b, left, right, source, smooth, sums, in_sem, out_sem):
    planes, rows = left.shape[0], left.shape[1]
    parts = source.shape[1]
    half = planes // 2
    me = lax.axis_index("gz")
    odd = me % 2

    def fetch(z):
        return [
            pltpu.make_async_copy(orbitals.at[pair_index[0, k], z], buffer.at[z], in_sem.at[k, z])
            for k, buffer in ((0, left), (1, right))
        ]

    for z in range(planes):
        for copy in fetch(z):
            copy.start()
    zero_pads(source, rows)
    zero_pads(smooth, rows)
    zero_planes(source, (0, planes + 1), rows)
    zero_planes(smooth, (0, 1, planes + 2, planes + 3), rows)
    matrices = restrict_matrices(parts * LANES, parts)

    for z in range(planes):
        for copy in fetch(z):
            copy.wait()

        for row in range(0, rows, 2 * ROWS):
            for h in range(parts):
                here = (z, pl.ds(row, 2 * ROWS), pl.ds(h * LANES, LANES))
                source[z + 1, h, pl.ds(PAD + row, 2 * ROWS), :] = left[here].astype(F32) * right[here].astype(F32)

    def keep(start, target, k):
        return pltpu.make_async_copy(source.at[pl.ds(start, half), :, pl.ds(PAD, rows), :], target, out_sem.at[k])

    kept = [keep(1 + half * (1 - odd), own_a, 0), keep(1 + half * odd, own_b, 1)]

    apply_planes(smooth, source, 1, planes + 1, 1, rows)

    def spread(target, origin):
        for h in range(parts):
            smooth[target, h, pl.ds(PAD, rows), :] = source[origin, h, pl.ds(PAD, rows), :] * NINTH

    @pl.when(me > 0)
    def _():
        spread(1, 1)

    @pl.when(me < size - 1)
    def _():
        spread(planes + 2, planes)

    for copy in kept:
        copy.start()

    def coarse(q, _):
        sums[q + 1] = restrict_pair(smooth, 2 * q + 2, rows, matrices)
        return 0

    lax.fori_loop(0, half, coarse, 0)
    low = [smooth[1, h, pl.ds(PAD + k, rows // 2, stride=2), :] for h in range(parts) for k in (-1, 0, 1, 2)]
    low_z = [smooth[2, h, pl.ds(PAD + k, rows // 2, stride=2), :] for h in range(parts) for k in (0, 1)]
    high = [smooth[planes + 2, h, pl.ds(PAD + k, rows // 2, stride=2), :] for h in range(parts) for k in (-1, 0, 1, 2)]
    high_z = [smooth[planes + 1, h, pl.ds(PAD + k, rows // 2, stride=2), :] for h in range(parts) for k in (0, 1)]

    def edge(inner, far):
        total = None
        for h in range(parts):
            i = inner[4 * h : 4 * h + 4]
            part = split_dot(i[1] + i[2], matrices[0][h])
            part += split_dot(i[0] + i[3] + (far[2 * h] + far[2 * h + 1]), matrices[1][h])
            total = part if total is None else total + part
        return total * (NINTH / 8.0)

    sums[0] = jnp.where(me > 0, edge(low, low_z), 0.0)
    sums[half + 1] = jnp.where(me < size - 1, edge(high, high_z), 0.0)

    three = (half + 2) // 2

    @pl.when(odd == 0)
    def _():
        coarse_a[...] = sums[pl.ds(three, three)]
        coarse_b[...] = sums[pl.ds(0, three)]

    @pl.when(odd == 1)
    def _():
        coarse_a[...] = sums[pl.ds(0, three)]
        coarse_b[...] = sums[pl.ds(three, three)]

    for copy in kept:
        copy.wait()


def middle_kernel(size, sent_a, sent_b, got_a, got_b, whole, next_a, next_b, packed, field, smooth):
    rows = sent_a.shape[1]
    planes = whole.shape[0] - 4
    me = lax.axis_index("gz")
    zero_pads(field, rows)
    zero_pads(smooth, rows)
    first, second = restrict_matrices(LANES, 1), restrict_matrices(LANES, 1, LANES // 2)

    def gather(own, low, high):
        centre = pl.ds(PAD, rows)
        n = planes
        for plane in range(n + 4):
            value = None
            if 1 <= plane <= n + 2:
                source, at = own[(plane - 1) // ((n + 2) // 2)], (plane - 1) % ((n + 2) // 2)
                value = source[at]
            if plane < 3:
                value = low[plane] if value is None else value + low[plane]
            if plane > n:
                value = high[plane - n - 1] if value is None else value + high[plane - n - 1]
            whole[plane] = value
            field[plane, 0, centre, :] = value

    @pl.when(me % 2 == 0)
    def _():
        gather((sent_b, sent_a), got_b, got_a)

    @pl.when(me % 2 == 1)
    def _():
        gather((sent_a, sent_b), got_a, got_b)

    apply_planes(smooth, field, jnp.where(me == 0, 2, 1), jnp.where(me == size - 1, planes + 2, planes + 3), 0, rows)

    @pl.when(me == 0)
    def _():
        zero_planes(smooth, (1,), rows)

    @pl.when(me == size - 1)
    def _():
        zero_planes(smooth, (planes + 2,), rows)

    packed[...] = restrict_pair(smooth, 2, rows, first) + restrict_pair(smooth, 4, rows, second)

    up, down = whole[pl.ds(1, 3)], whole[pl.ds(planes, 3)]

    @pl.when(me % 2 == 0)
    def _():
        next_a[...] = up
        next_b[...] = down

    @pl.when(me % 2 == 1)
    def _():
        next_a[...] = down
        next_b[...] = up


def packed_apply(ref, block, rows):
    centre = ref[block, pl.ds(PAD, rows), :]
    lane = iota((rows, LANES), 1)
    half = LANES // 2
    total = ref[block, pl.ds(PAD - 1, rows), :] + ref[block, pl.ds(PAD + 1, rows), :]
    other = jnp.where(lane >= half, ref[block - 1, pl.ds(PAD, rows), :], ref[block + 1, pl.ds(PAD, rows), :])
    total += pltpu.roll(centre + other, half, 1)
    total += jnp.where((lane & (half - 1)) == 0, 0.0, pltpu.roll(centre, 1, 1))
    total += jnp.where((lane & (half - 1)) == half - 1, 0.0, pltpu.roll(centre, LANES - 1, 1))
    return centre * THIRD + total * NINTH


def last_apply(ref, plane, rows, width):
    centre = ref[plane, pl.ds(PAD, rows), :]
    lane = iota((rows, LANES), 1)
    total = ref[plane, pl.ds(PAD - 1, rows), :] + ref[plane, pl.ds(PAD + 1, rows), :]
    total += ref[plane - 1, pl.ds(PAD, rows), :] + ref[plane + 1, pl.ds(PAD, rows), :]
    total += pltpu.roll(centre, 1, 1) + pltpu.roll(centre, LANES - 1, 1)
    return jnp.where(lane < width, centre * THIRD + total * NINTH, 0.0)


def coarse_levels(size, source, result, blocks, smooth, bottom, spare):
    rows = source.shape[1] - 2 * PAD
    half = rows // 2
    width = LANES // 4
    c2, c3 = scale(2), scale(3)
    row, column = iota((LANES, LANES), 0), iota((LANES, LANES), 1)
    gather = to_bf16(((row & (LANES // 2 - 1)) >> 1) == column)
    scatter = to_bf16(((column & (LANES // 2 - 1)) >> 1) == row)
    centre = pl.ds(PAD, rows)
    inner = pl.ds(PAD, half)

    for b in range(1, size + 1):
        smooth[b, centre, :] = packed_apply(source, b, rows)
    for b in range(1, size + 1):
        spare[b] = packed_apply(smooth, b, rows)
    for b in range(1, size + 1):
        pairs = spare[b, pl.ds(0, half, stride=2), :] + spare[b, pl.ds(1, half, stride=2), :]
        value = split_dot(pairs, gather) * (c3 / 8.0)
        bottom[2, b, inner, :] = value
        bottom[0, b, inner, :] = value
    now = 0
    for _ in range(SWEEPS - 1):
        for b in range(1, size + 1):
            bottom[1 - now, b, inner, :] = last_apply(bottom.at[now], b, half, width) + bottom[2, b, inner, :]
        now = 1 - now
    for b in range(1, size + 1):
        value = split_dot(bottom[now, b, inner, :], scatter)
        spare[b, pl.ds(0, half, stride=2), :] = value
        spare[b, pl.ds(1, half, stride=2), :] = value
    for b in range(1, size + 1):
        source_b = source[b, centre, :] * c2
        blocks[b, centre, :] = source_b + smooth[b, centre, :] * c2 + spare[b]
    for b in range(1, size + 1):
        smooth[b, centre, :] = packed_apply(blocks, b, rows) + source[b, centre, :] * c2
    for b in range(1, size + 1):
        result[b, centre, :] = packed_apply(smooth, b, rows) + source[b, centre, :] * c2


def last_kernel(
    size, partners, cells, own_a, own_b, got_a, got_b, whole, next_a, next_b, *rest
):
    arrived = rest[: len(partners)]
    weight, potential, sums = rest[len(partners) : len(partners) + 3]
    scratch = rest[len(partners) + 3 :]
    (field, first, second, third, grown, mid, mid_first, mid_second, mid_third, mid_grown) = scratch[:10]
    (low_source, low_result, low_blocks, low_smooth, bottom, spare, in_sem, out_sem) = scratch[10:]
    parts, rows = own_a.shape[1], own_a.shape[2]
    half = own_a.shape[0]
    planes = 2 * half
    mid_rows = whole.shape[1]
    mid_planes = whole.shape[0] - 4
    low_rows = arrived[0].shape[0]
    me = lax.axis_index("gz")
    odd = me % 2
    is_first, is_last = me == 0, me == size - 1

    def bring(k, origin, plane):
        return pltpu.make_async_copy(origin, field.at[pl.ds(plane, half), :, pl.ds(PAD, rows), :], in_sem.at[k])

    copies = [
        bring(0, own_a, half + half * (1 - odd)),
        bring(1, own_b, half + half * odd),
        bring(2, got_a, 3 * half * (1 - odd)),
        bring(3, got_b, 3 * half * odd),
    ]
    for copy in copies:
        copy.start()

    blank = jnp.zeros((PAD, LANES), F32)
    for ref in (field, first, second, third):
        zero_pads(ref, rows)
    for ref in (mid, mid_first, mid_second):
        zero_pads(ref, mid_rows)
    for ref in (low_source, low_blocks, low_smooth):
        for b in range(size + 2):
            ref[b, pl.ds(0, PAD), :] = blank
            ref[b, pl.ds(PAD + low_rows, PAD), :] = blank
        for b in (0, size + 1):
            ref[b, pl.ds(PAD, low_rows), :] = jnp.zeros((low_rows, LANES), F32)
    for k in range(2):
        for b in range(size + 2):
            bottom[k, b, pl.ds(0, PAD), :] = blank
            bottom[k, b, pl.ds(PAD + low_rows // 2, PAD), :] = blank
        for b in (0, size + 1):
            bottom[k, b] = jnp.zeros(bottom.shape[2:], F32)
    for b in (0, size + 1):
        low_result[b, pl.ds(PAD, low_rows), :] = jnp.zeros((low_rows, LANES), F32)

    for partner, ref in zip(partners, arrived):
        low_source[jnp.bitwise_xor(me, partner) + 1, pl.ds(PAD, low_rows), :] = ref[...]

    coarse_levels(size, low_source, low_result, low_blocks, low_smooth, bottom, spare)

    edge = 3
    middle = pl.ds(PAD, mid_rows)
    for plane in range(mid_planes + 4):
        mid[edge + plane, 0, middle, :] = whole[plane]

    def sides(low, high):
        for k in range(edge):
            mid[k, 0, middle, :] = low[k]
            mid[edge + mid_planes + 4 + k, 0, middle, :] = high[k]

    @pl.when(odd == 0)
    def _():
        sides(next_b, next_a)

    @pl.when(odd == 1)
    def _():
        sides(next_a, next_b)

    row, column = iota((LANES, LANES), 0), iota((LANES, LANES), 1)
    for k in range(3):
        block = low_result[me + k, pl.ds(PAD, low_rows), :]
        for side in range(2):
            matrix = to_bf16((column >> 1) + side * (LANES // 2) == row)
            value = split_dot(block, matrix)
            mid_grown[2 * k + side, 0, pl.ds(0, low_rows, stride=2), :] = value
            mid_grown[2 * k + side, 0, pl.ds(1, low_rows, stride=2), :] = value

    def start(dst, src, grown_ref, first_plane, last_plane, shift, offset, level, n):
        c = scale(level)

        def plane(z, _):
            for r in range(0, n, ROWS):
                centre, total = neighbours(src, z, r, ROWS)
                for h in range(len(centre)):
                    value = centre[h] * (c * (1.0 + THIRD)) + total[h] * (c * NINTH)
                    dst[z + shift, h, pl.ds(PAD + r, ROWS), :] = value + grown_ref[(z + offset) >> 1, h, pl.ds(r, ROWS), :]
            return 0

        lax.fori_loop(first_plane, last_plane, plane, 0)

    def again(dst, src, source, first_plane, last_plane, shift, offset, level, n):
        c = scale(level)

        def plane(z, _):
            for r in range(0, n, ROWS):
                centre, total = neighbours(src, z, r, ROWS)
                for h in range(len(centre)):
                    value = centre[h] * THIRD + total[h] * NINTH
                    dst[z + shift, h, pl.ds(PAD + r, ROWS), :] = value + source[z + offset, h, pl.ds(PAD + r, ROWS), :] * c
            return 0

        lax.fori_loop(first_plane, last_plane, plane, 0)

    def blank_outside(ref, halo, inside, n):
        @pl.when(is_first)
        def _():
            zero_planes(ref, range(halo), n)

        @pl.when(is_last)
        def _():
            zero_planes(ref, range(halo + inside, 2 * halo + inside), n)

    def span(halo, inside):
        return jnp.where(is_first, halo, 0), jnp.where(is_last, halo + inside, 2 * halo + inside)

    n = mid_planes
    low, high = span(4, n)
    start(mid_first, mid, mid_grown, low + 1, high + 1, -1, -1, 1, mid_rows)
    blank_outside(mid_first, 4, n, mid_rows)
    low, high = span(3, n)
    again(mid_second, mid_first, mid, low + 1, high + 1, -1, 1, 1, mid_rows)
    blank_outside(mid_second, 3, n, mid_rows)
    low, high = span(2, n)

    spread = [to_bf16((column + h * LANES) >> 1 == row) for h in range(parts)]
    c1 = scale(1)

    def correct(z, _):
        for r in range(0, mid_rows, ROWS):
            centre, total = neighbours(mid_second, z + 1, r, ROWS)
            mid_third[pl.ds(r, ROWS), :] = centre[0] * THIRD + total[0] * NINTH + mid[z + 3, 0, pl.ds(PAD + r, ROWS), :] * c1
        value = mid_third[...]
        for h in range(parts):
            wide = split_dot(value, spread[h])
            grown[z, h, pl.ds(0, mid_rows, stride=2), :] = wide
            grown[z, h, pl.ds(1, mid_rows, stride=2), :] = wide
        return 0

    lax.fori_loop(low, high, correct, 0)

    for copy in copies:
        copy.wait()

    n = planes
    low, high = span(3, n)
    start(first, field, grown, low + 1, high + 1, -1, 0, 0, rows)
    blank_outside(first, 3, n, rows)
    low, high = span(2, n)
    again(second, first, field, low + 1, high + 1, -1, 1, 0, rows)
    blank_outside(second, 2, n, rows)
    low, high = span(1, n)
    again(third, second, field, low + 1, high + 1, -1, 2, 0, rows)
    blank_outside(third, 1, n, rows)

    def give(z, h):
        target = potential.at[0, z, :, pl.ds(h * LANES, LANES)]
        return pltpu.make_async_copy(third.at[z + 1, h, pl.ds(PAD, rows), :], target, out_sem.at[z, h])

    for z in range(n):
        for h in range(parts):
            give(z, h).start()

    def final(z, totals):
        squares, products = totals
        for r in range(0, rows, ROWS):
            centre, total = neighbours(third, z + 1, r, ROWS)
            for h in range(parts):
                f = field[z + half, h, pl.ds(PAD + r, ROWS), :]
                rest_of = f - 6.0 * centre[h] + total[h]
                squares += jnp.sum((rest_of * rest_of).reshape(ROWS // 8, 8, LANES), axis=0)
                products += jnp.sum((f * centre[h]).reshape(ROWS // 8, 8, LANES), axis=0)
        return squares, products

    squares, products = lax.fori_loop(0, n, final, (jnp.zeros((8, LANES), F32),) * 2)
    products = products * (weight[0] * (-0.5 / cells))
    both = jnp.concatenate([jnp.sum(squares, axis=0, keepdims=True), jnp.sum(products, axis=0, keepdims=True)], axis=0)
    sums[...] = jnp.broadcast_to(both[None], sums.shape)
    for z in range(n):
        for h in range(parts):
            give(z, h).wait()


def exchange(value, pairs):
    return lax.ppermute(value, "gz", [move for a, b in pairs for move in ((a, b), (b, a))])


def params(mib):
    return pltpu.CompilerParams(vmem_limit_bytes=mib << 20)


def per_device(orbitals, pair_index, pair_weight):
    size = lax.axis_size("gz")
    groups = lax.axis_size("pair")
    _, planes, rows, columns = orbitals.shape
    parts = columns // LANES
    assert planes == 8 and columns == 2 * LANES and rows % (4 * ROWS) == 0 and pair_index.shape[0] == 1 and size % 2 == 0
    half, quarter = planes // 2, planes // 4
    mid_rows, low_rows = rows // 2, rows // 4
    tall, mid_tall, low_tall = rows + 2 * PAD, mid_rows + 2 * PAD, low_rows + 2 * PAD
    inner = [(i, i + 1) for i in range(0, size, 2)]
    outer = [(i, i + 1) for i in range(1, size - 1, 2)]

    def shape(*dims):
        return jax.ShapeDtypeStruct(dims, F32)

    def scratch(*dims):
        return pltpu.VMEM(dims, F32)

    three = (half + 2) // 2
    own_a, own_b, coarse_a, coarse_b = pl.pallas_call(
        functools.partial(fine_kernel, size),
        out_shape=[shape(half, parts, rows, LANES)] * 2 + [shape(three, mid_rows, LANES)] * 2,
        in_specs=[ANY, SMEM],
        out_specs=[ANY, ANY, VMEM, VMEM],
        scratch_shapes=[
            pltpu.VMEM((planes, rows, columns), orbitals.dtype),
            pltpu.VMEM((planes, rows, columns), orbitals.dtype),
            scratch(planes + 2, parts, tall, LANES),
            scratch(planes + 4, parts, tall, LANES),
            scratch(half + 2, mid_rows, LANES),
            pltpu.SemaphoreType.DMA((2, planes)),
            pltpu.SemaphoreType.DMA((2,)),
        ],
        compiler_params=params(24),
        name="fine",
    )(orbitals, pair_index)

    coarse_got_a = exchange(coarse_a, inner)
    coarse_got_b = exchange(coarse_b, outer)
    own_got_a = exchange(own_a, inner)
    own_got_b = exchange(own_b, outer)

    whole, next_a, next_b, packed = pl.pallas_call(
        functools.partial(middle_kernel, size),
        out_shape=[shape(half + 4, mid_rows, LANES)] + [shape(3, mid_rows, LANES)] * 2 + [shape(low_rows, LANES)],
        in_specs=[VMEM] * 4,
        out_specs=[VMEM] * 4,
        scratch_shapes=[scratch(half + 4, 1, mid_tall, LANES)] * 2,
        compiler_params=params(8),
        name="middle",
    )(coarse_a, coarse_b, coarse_got_a, coarse_got_b)

    partners = list(range(0, size, 2))
    arrived = [packed] + [exchange(packed, [(i, i ^ k) for i in range(size) if i < i ^ k]) for k in partners[1:]]
    arrived += [exchange(value, inner) for value in arrived]
    partners += [k ^ 1 for k in partners]
    next_got_a = exchange(next_a, inner)
    next_got_b = exchange(next_b, outer)

    cells = planes * size * rows * columns
    potential, sums = pl.pallas_call(
        functools.partial(last_kernel, size, tuple(partners), cells),
        out_shape=[shape(1, planes, rows, columns), shape(size * groups, 2, LANES)],
        in_specs=[ANY] * 4 + [VMEM] * (3 + len(partners)) + [SMEM],
        out_specs=[ANY, VMEM],
        scratch_shapes=[
            scratch(planes + 8, parts, tall, LANES),
            scratch(planes + 6, parts, tall, LANES),
            scratch(planes + 4, parts, tall, LANES),
            scratch(planes + 2, parts, tall, LANES),
            scratch(half + 4, parts, rows, LANES),
            scratch(half + 10, 1, mid_tall, LANES),
            scratch(half + 8, 1, mid_tall, LANES),
            scratch(half + 6, 1, mid_tall, LANES),
            scratch(mid_rows, LANES),
            scratch(6, 1, mid_rows, LANES),
            scratch(size + 2, low_tall, LANES),
            scratch(size + 2, low_tall, LANES),
            scratch(size + 2, low_tall, LANES),
            scratch(size + 2, low_tall, LANES),
            scratch(3, size + 2, low_rows // 2 + 2 * PAD, LANES),
            scratch(size + 2, low_rows, LANES),
            pltpu.SemaphoreType.DMA((4,)),
            pltpu.SemaphoreType.DMA((planes, parts)),
        ],
        compiler_params=params(32),
        name="last",
    )(own_a, own_b, own_got_a, own_got_b, whole, next_got_a, next_got_b, *arrived, pair_weight)

    everyone = lax.all_to_all(sums, ("gz", "pair"), 0, 0).reshape(size, groups, 2, LANES)
    mine = iota((size, groups, LANES), 1) == lax.axis_index("pair")
    squares = jnp.sum(jnp.where(mine, everyone[:, :, 0], 0.0))
    energy = jnp.sum(everyone[:, :, 1])
    return (potential, jnp.sqrt(squares / cells).reshape(1), energy.reshape(1))


def solution(mesh):
    return jax.shard_map(
        per_device,
        mesh=mesh,
        in_specs=(P(None, "gz", None, None), P("pair", None), P("pair")),
        out_specs=(P("pair", "gz", None, None), P("pair"), P()),
        check_vma=False,
    )
```

```python
import functools

import jax
import jax.numpy as jnp
from jax import lax
from jax.experimental import pallas as pl
from jax.experimental.pallas import tpu as pltpu
from jax.sharding import PartitionSpec as P


LANES = 128
PAD = 8
SWEEPS = 8
ROWS = 32
THIRD = 1.0 / 3.0
NINTH = 1.0 / 9.0
F32 = jnp.float32
BF16 = jnp.bfloat16
ANY = pl.BlockSpec(memory_space=pl.ANY)
VMEM = pl.BlockSpec(memory_space=pltpu.VMEM)
SMEM = pl.BlockSpec(memory_space=pltpu.SMEM)
HBM = pl.BlockSpec(memory_space=pltpu.HBM)


def scale(level):
    return 4.0**level / 9.0


def iota(shape, dim):
    return lax.broadcasted_iota(jnp.int32, shape, dim)


def split_dot(value, matrix):
    high = value.astype(BF16)
    low = (value - high.astype(F32)).astype(BF16)
    return jnp.dot(high, matrix, preferred_element_type=F32) + jnp.dot(low, matrix, preferred_element_type=F32)


def to_bf16(mask, value=1.0):
    return jnp.where(mask, value, 0.0).astype(BF16)


def neighbours(ref, z, row, rows):
    parts = ref.shape[1]
    centre = [ref[z, h, pl.ds(PAD + row, rows), :] for h in range(parts)]
    lane = iota((rows, LANES), 1)
    after = [pltpu.roll(c, 1, 1) for c in centre]
    before = [pltpu.roll(c, LANES - 1, 1) for c in centre]
    sums = []
    for h in range(parts):
        total = ref[z, h, pl.ds(PAD + row - 1, rows), :] + ref[z, h, pl.ds(PAD + row + 1, rows), :]
        total += ref[z - 1, h, pl.ds(PAD + row, rows), :] + ref[z + 1, h, pl.ds(PAD + row, rows), :]
        total += jnp.where(lane == 0, after[h - 1] if h else 0.0, after[h])
        total += jnp.where(lane == LANES - 1, before[h + 1] if h + 1 < parts else 0.0, before[h])
        sums.append(total)
    return centre, sums


def zero_pads(ref, rows):
    blank = jnp.zeros((PAD, LANES), F32)

    def plane(z, _):
        for h in range(ref.shape[1]):
            ref[z, h, pl.ds(0, PAD), :] = blank
            ref[z, h, pl.ds(PAD + rows, PAD), :] = blank
        return 0

    lax.fori_loop(0, ref.shape[0], plane, 0)


def zero_planes(ref, planes, rows):
    for z in planes:
        for h in range(ref.shape[1]):
            ref[z, h, pl.ds(PAD, rows), :] = jnp.zeros((rows, LANES), F32)


def apply_planes(dst, src, first, last, shift, rows):
    def plane(z, _):
        for row in range(0, rows, ROWS):
            centre, sums = neighbours(src, z, row, ROWS)
            for h in range(len(centre)):
                dst[z + shift, h, pl.ds(PAD + row, ROWS), :] = centre[h] * THIRD + sums[h] * NINTH
        return 0

    lax.fori_loop(first, last, plane, 0)


def restrict_pair(ref, z, rows, matrices):
    total = None
    half = rows // 2
    for h in range(ref.shape[1]):

        def at(plane, offset):
            return ref[plane, h, pl.ds(PAD + offset, half, stride=2), :]

        inner = [at(z, k) + at(z + 1, k) for k in (-1, 0, 1, 2)]
        pair = inner[1] + inner[2]
        outer = inner[0] + inner[3] + (at(z - 1, 0) + at(z - 1, 1)) + (at(z + 2, 0) + at(z + 2, 1))
        part = split_dot(pair, matrices[0][h]) + split_dot(outer, matrices[1][h])
        total = part if total is None else total + part
    return total * (NINTH / 8.0)


def restrict_matrices(width, parts, out_shift=0):
    stencil, plain = [], []
    for h in range(parts):
        row = iota((LANES, LANES), 0) + h * LANES
        column = iota((LANES, LANES), 1) - out_shift
        inside = (column >= 0) & (column < width // 2)
        own = (row >> 1) == column
        beside = (row == 2 * column - 1) | (row == 2 * column + 2)
        stencil.append(jnp.where(inside & own, 6.0, jnp.where(inside & beside, 1.0, 0.0)).astype(BF16))
        plain.append(to_bf16(inside & own))
    return stencil, plain


def fine_kernel(size, orbitals, pair_index, own_a, own_b, coarse_a, coarse_b, left, right, source, smooth, sums, in_sem, out_sem):
    planes, rows = left.shape[0], left.shape[1]
    parts = source.shape[1]
    half = planes // 2
    me = lax.axis_index("gz")
    odd = me % 2

    def fetch(z):
        return [
            pltpu.make_async_copy(orbitals.at[pair_index[k], z], buffer.at[z], in_sem.at[k, z])
            for k, buffer in ((0, left), (1, right))
        ]

    for z in range(planes):
        for copy in fetch(z):
            copy.start()
    zero_pads(source, rows)
    zero_pads(smooth, rows)
    zero_planes(source, (0, planes + 1), rows)
    zero_planes(smooth, (0, 1, planes + 2, planes + 3), rows)
    matrices = restrict_matrices(parts * LANES, parts)

    for z in range(planes):
        for copy in fetch(z):
            copy.wait()

        for row in range(0, rows, 2 * ROWS):
            for h in range(parts):
                here = (z, pl.ds(row, 2 * ROWS), pl.ds(h * LANES, LANES))
                source[z + 1, h, pl.ds(PAD + row, 2 * ROWS), :] = left[here].astype(F32) * right[here].astype(F32)

    def keep(start, target, k):
        return pltpu.make_async_copy(source.at[pl.ds(start, half), :, pl.ds(PAD, rows), :], target, out_sem.at[k])

    kept = [keep(1 + half * (1 - odd), own_a, 0), keep(1 + half * odd, own_b, 1)]

    apply_planes(smooth, source, 1, planes + 1, 1, rows)

    def spread(target, origin):
        for h in range(parts):
            smooth[target, h, pl.ds(PAD, rows), :] = source[origin, h, pl.ds(PAD, rows), :] * NINTH

    @pl.when(me > 0)
    def _():
        spread(1, 1)

    @pl.when(me < size - 1)
    def _():
        spread(planes + 2, planes)

    for copy in kept:
        copy.start()

    def coarse(q, _):
        sums[q + 1] = restrict_pair(smooth, 2 * q + 2, rows, matrices)
        return 0

    lax.fori_loop(0, half, coarse, 0)
    low = [smooth[1, h, pl.ds(PAD + k, rows // 2, stride=2), :] for h in range(parts) for k in (-1, 0, 1, 2)]
    low_z = [smooth[2, h, pl.ds(PAD + k, rows // 2, stride=2), :] for h in range(parts) for k in (0, 1)]
    high = [smooth[planes + 2, h, pl.ds(PAD + k, rows // 2, stride=2), :] for h in range(parts) for k in (-1, 0, 1, 2)]
    high_z = [smooth[planes + 1, h, pl.ds(PAD + k, rows // 2, stride=2), :] for h in range(parts) for k in (0, 1)]

    def edge(inner, far):
        total = None
        for h in range(parts):
            i = inner[4 * h : 4 * h + 4]
            part = split_dot(i[1] + i[2], matrices[0][h])
            part += split_dot(i[0] + i[3] + (far[2 * h] + far[2 * h + 1]), matrices[1][h])
            total = part if total is None else total + part
        return total * (NINTH / 8.0)

    sums[0] = jnp.where(me > 0, edge(low, low_z), 0.0)
    sums[half + 1] = jnp.where(me < size - 1, edge(high, high_z), 0.0)

    three = (half + 2) // 2

    @pl.when(odd == 0)
    def _():
        coarse_a[...] = sums[pl.ds(three, three)]
        coarse_b[...] = sums[pl.ds(0, three)]

    @pl.when(odd == 1)
    def _():
        coarse_a[...] = sums[pl.ds(0, three)]
        coarse_b[...] = sums[pl.ds(three, three)]

    for copy in kept:
        copy.wait()


def middle_kernel(size, sent_a, sent_b, got_a, got_b, whole, next_a, next_b, packed, field, smooth):
    rows = sent_a.shape[1]
    planes = whole.shape[0] - 4
    me = lax.axis_index("gz")
    zero_pads(field, rows)
    zero_pads(smooth, rows)
    first, second = restrict_matrices(LANES, 1), restrict_matrices(LANES, 1, LANES // 2)

    def gather(own, low, high):
        centre = pl.ds(PAD, rows)
        n = planes
        for plane in range(n + 4):
            value = None
            if 1 <= plane <= n + 2:
                source, at = own[(plane - 1) // ((n + 2) // 2)], (plane - 1) % ((n + 2) // 2)
                value = source[at]
            if plane < 3:
                value = low[plane] if value is None else value + low[plane]
            if plane > n:
                value = high[plane - n - 1] if value is None else value + high[plane - n - 1]
            whole[plane] = value
            field[plane, 0, centre, :] = value

    @pl.when(me % 2 == 0)
    def _():
        gather((sent_b, sent_a), got_b, got_a)

    @pl.when(me % 2 == 1)
    def _():
        gather((sent_a, sent_b), got_a, got_b)

    apply_planes(smooth, field, jnp.where(me == 0, 2, 1), jnp.where(me == size - 1, planes + 2, planes + 3), 0, rows)

    @pl.when(me == 0)
    def _():
        zero_planes(smooth, (1,), rows)

    @pl.when(me == size - 1)
    def _():
        zero_planes(smooth, (planes + 2,), rows)

    packed[...] = restrict_pair(smooth, 2, rows, first) + restrict_pair(smooth, 4, rows, second)

    up, down = whole[pl.ds(1, 3)], whole[pl.ds(planes, 3)]

    @pl.when(me % 2 == 0)
    def _():
        next_a[...] = up
        next_b[...] = down

    @pl.when(me % 2 == 1)
    def _():
        next_a[...] = down
        next_b[...] = up


def packed_apply(ref, block, rows):
    centre = ref[block, pl.ds(PAD, rows), :]
    lane = iota((rows, LANES), 1)
    half = LANES // 2
    total = ref[block, pl.ds(PAD - 1, rows), :] + ref[block, pl.ds(PAD + 1, rows), :]
    other = jnp.where(lane >= half, ref[block - 1, pl.ds(PAD, rows), :], ref[block + 1, pl.ds(PAD, rows), :])
    total += pltpu.roll(centre + other, half, 1)
    total += jnp.where((lane & (half - 1)) == 0, 0.0, pltpu.roll(centre, 1, 1))
    total += jnp.where((lane & (half - 1)) == half - 1, 0.0, pltpu.roll(centre, LANES - 1, 1))
    return centre * THIRD + total * NINTH


def last_apply(ref, plane, rows, width):
    centre = ref[plane, pl.ds(PAD, rows), :]
    lane = iota((rows, LANES), 1)
    total = ref[plane, pl.ds(PAD - 1, rows), :] + ref[plane, pl.ds(PAD + 1, rows), :]
    total += ref[plane - 1, pl.ds(PAD, rows), :] + ref[plane + 1, pl.ds(PAD, rows), :]
    total += pltpu.roll(centre, 1, 1) + pltpu.roll(centre, LANES - 1, 1)
    return jnp.where(lane < width, centre * THIRD + total * NINTH, 0.0)


def coarse_levels(size, source, result, blocks, smooth, bottom, spare):
    rows = source.shape[1] - 2 * PAD
    half = rows // 2
    width = LANES // 4
    c2, c3 = scale(2), scale(3)
    row, column = iota((LANES, LANES), 0), iota((LANES, LANES), 1)
    gather = to_bf16(((row & (LANES // 2 - 1)) >> 1) == column)
    scatter = to_bf16(((column & (LANES // 2 - 1)) >> 1) == row)
    centre = pl.ds(PAD, rows)
    inner = pl.ds(PAD, half)

    for b in range(1, size + 1):
        smooth[b, centre, :] = packed_apply(source, b, rows)
    for b in range(1, size + 1):
        spare[b] = packed_apply(smooth, b, rows)
    for b in range(1, size + 1):
        pairs = spare[b, pl.ds(0, half, stride=2), :] + spare[b, pl.ds(1, half, stride=2), :]
        value = split_dot(pairs, gather) * (c3 / 8.0)
        bottom[2, b, inner, :] = value
        bottom[0, b, inner, :] = value
    now = 0
    for _ in range(SWEEPS - 1):
        for b in range(1, size + 1):
            bottom[1 - now, b, inner, :] = last_apply(bottom.at[now], b, half, width) + bottom[2, b, inner, :]
        now = 1 - now
    for b in range(1, size + 1):
        value = split_dot(bottom[now, b, inner, :], scatter)
        spare[b, pl.ds(0, half, stride=2), :] = value
        spare[b, pl.ds(1, half, stride=2), :] = value
    for b in range(1, size + 1):
        source_b = source[b, centre, :] * c2
        blocks[b, centre, :] = source_b + smooth[b, centre, :] * c2 + spare[b]
    for b in range(1, size + 1):
        smooth[b, centre, :] = packed_apply(blocks, b, rows) + source[b, centre, :] * c2
    for b in range(1, size + 1):
        result[b, centre, :] = packed_apply(smooth, b, rows) + source[b, centre, :] * c2


def bring_all(pairs, sem):
    copies = [pltpu.make_async_copy(origin, target, sem.at[k]) for k, (origin, target) in enumerate(pairs)]
    for copy in copies:
        copy.start()
    return copies


def start_level(dst, src, grown, planes, shift, offset, level, rows):
    c = scale(level)

    def plane(z, _):
        for r in range(0, rows, ROWS):
            centre, total = neighbours(src, z, r, ROWS)
            for h in range(len(centre)):
                value = centre[h] * (c * (1.0 + THIRD)) + total[h] * (c * NINTH)
                dst[z + shift, h, pl.ds(PAD + r, ROWS), :] = value + grown[(z + offset) >> 1, h, pl.ds(r, ROWS), :]
        return 0

    lax.fori_loop(*planes, plane, 0)


def sweep_level(dst, src, source, planes, shift, offset, level, rows):
    c = scale(level)

    def plane(z, _):
        for r in range(0, rows, ROWS):
            centre, total = neighbours(src, z, r, ROWS)
            for h in range(len(centre)):
                value = centre[h] * THIRD + total[h] * NINTH
                dst[z + shift, h, pl.ds(PAD + r, ROWS), :] = value + source[z + offset, h, pl.ds(PAD + r, ROWS), :] * c
        return 0

    lax.fori_loop(*planes, plane, 0)


def span(me, size, halo, inside, shift=0):
    low = jnp.where(me == 0, halo, 0)
    high = jnp.where(me == size - 1, halo + inside, 2 * halo + inside)
    return low + shift, high + shift


def blank_outside(ref, me, size, halo, inside, rows):
    @pl.when(me == 0)
    def _():
        zero_planes(ref, range(halo), rows)

    @pl.when(me == size - 1)
    def _():
        zero_planes(ref, range(halo + inside, 2 * halo + inside), rows)


def low_kernel(size, partners, whole, next_a, next_b, *rest):
    arrived, (result,) = rest[: len(partners)], rest[len(partners) : len(partners) + 1]
    (mid, first, second, _, grown) = rest[len(partners) + 1 : len(partners) + 6]
    (low_source, low_result, low_blocks, low_smooth, bottom, spare, low_sem, mid_sem) = rest[len(partners) + 6 :]
    rows = whole.shape[1]
    planes = whole.shape[0] - 4
    low_rows = arrived[0].shape[0]
    me = lax.axis_index("gz")
    odd = me % 2
    blank = jnp.zeros((PAD, LANES), F32)
    inner = pl.ds(PAD, low_rows)
    middle = pl.ds(PAD, rows)
    edge = 3

    blocks = [
        (ref, low_source.at[jnp.bitwise_xor(me, partner) + 1, inner]) for partner, ref in zip(partners, arrived)
    ]
    low_copies = bring_all(blocks, low_sem)
    top = edge + planes + 4
    mid_copies = bring_all(
        [
            (whole, mid.at[pl.ds(edge, planes + 4), 0, middle]),
            (next_a, mid.at[pl.ds(top * (1 - odd), edge), 0, middle]),
            (next_b, mid.at[pl.ds(top * odd, edge), 0, middle]),
        ],
        mid_sem,
    )

    for ref in (mid, first, second):
        zero_pads(ref, rows)
    for ref in (low_source, low_blocks, low_smooth):
        for b in range(size + 2):
            ref[b, pl.ds(0, PAD), :] = blank
            ref[b, pl.ds(PAD + low_rows, PAD), :] = blank
        for b in (0, size + 1):
            ref[b, inner, :] = jnp.zeros((low_rows, LANES), F32)
    for k in range(2):
        for b in range(size + 2):
            bottom[k, b, pl.ds(0, PAD), :] = blank
            bottom[k, b, pl.ds(PAD + low_rows // 2, PAD), :] = blank
        for b in (0, size + 1):
            bottom[k, b] = jnp.zeros(bottom.shape[2:], F32)
    for b in (0, size + 1):
        low_result[b, inner, :] = jnp.zeros((low_rows, LANES), F32)
    blank_outside(first, me, size, 4, planes, rows)
    blank_outside(second, me, size, 3, planes, rows)

    for copy in low_copies:
        copy.wait()
    coarse_levels(size, low_source, low_result, low_blocks, low_smooth, bottom, spare)

    row, column = iota((LANES, LANES), 0), iota((LANES, LANES), 1)
    for k in range(3):
        block = low_result[me + k, inner, :]
        for side in range(2):
            value = split_dot(block, to_bf16((column >> 1) + side * (LANES // 2) == row))
            grown[2 * k + side, 0, pl.ds(0, low_rows, stride=2), :] = value
            grown[2 * k + side, 0, pl.ds(1, low_rows, stride=2), :] = value

    for copy in mid_copies:
        copy.wait()
    start_level(first, mid, grown, span(me, size, 4, planes, 1), -1, -1, 1, rows)
    sweep_level(second, first, mid, span(me, size, 3, planes, 1), -1, 1, 1, rows)
    c1 = scale(1)

    def last(z, _):
        for r in range(0, rows, ROWS):
            centre, total = neighbours(second, z + 1, r, ROWS)
            value = centre[0] * THIRD + total[0] * NINTH
            result[z, pl.ds(r, ROWS), :] = value + mid[z + 3, 0, pl.ds(PAD + r, ROWS), :] * c1
        return 0

    lax.fori_loop(*span(me, size, 2, planes), last, 0)


def top_kernel(size, cells, own_a, own_b, got_a, got_b, correction, weight, potential, sums, *scratch):
    field, first, second, third, grown, in_sem, out_sem = scratch
    half, parts, rows = own_a.shape[0], own_a.shape[1], own_a.shape[2]
    planes = 2 * half
    mid_rows = correction.shape[1]
    me = lax.axis_index("gz")
    odd = me % 2

    def into(plane):
        return field.at[pl.ds(plane, half), :, pl.ds(PAD, rows), :]

    copies = bring_all(
        [
            (own_a, into(half + half * (1 - odd))),
            (own_b, into(half + half * odd)),
            (got_a, into(3 * half * (1 - odd))),
            (got_b, into(3 * half * odd)),
        ],
        in_sem,
    )
    for ref in (field, first, second, third):
        zero_pads(ref, rows)
    blank_outside(first, me, size, 3, planes, rows)
    blank_outside(second, me, size, 2, planes, rows)
    blank_outside(third, me, size, 1, planes, rows)

    row, column = iota((LANES, LANES), 0), iota((LANES, LANES), 1)
    spread = [to_bf16((column + h * LANES) >> 1 == row) for h in range(parts)]

    def widen(z, _):
        value = correction[z]
        for h in range(parts):
            wide = split_dot(value, spread[h])
            grown[z, h, pl.ds(0, mid_rows, stride=2), :] = wide
            grown[z, h, pl.ds(1, mid_rows, stride=2), :] = wide
        return 0

    lax.fori_loop(*span(me, size, 2, half), widen, 0)

    for copy in copies:
        copy.wait()
    start_level(first, field, grown, span(me, size, 3, planes, 1), -1, 0, 0, rows)
    sweep_level(second, first, field, span(me, size, 2, planes, 1), -1, 1, 0, rows)
    sweep_level(third, second, field, span(me, size, 1, planes, 1), -1, 2, 0, rows)

    def give(z, h):
        target = potential.at[0, z, :, pl.ds(h * LANES, LANES)]
        return pltpu.make_async_copy(third.at[z + 1, h, pl.ds(PAD, rows), :], target, out_sem.at[z, h])

    for z in range(planes):
        for h in range(parts):
            give(z, h).start()

    def final(z, totals):
        squares, products = totals
        for r in range(0, rows, ROWS):
            centre, total = neighbours(third, z + 1, r, ROWS)
            for h in range(parts):
                f = field[z + half, h, pl.ds(PAD + r, ROWS), :]
                remain = f - 6.0 * centre[h] + total[h]
                squares += jnp.sum((remain * remain).reshape(ROWS // 8, 8, LANES), axis=0)
                products += jnp.sum((f * centre[h]).reshape(ROWS // 8, 8, LANES), axis=0)
        return squares, products

    squares, products = lax.fori_loop(0, planes, final, (jnp.zeros((8, LANES), F32),) * 2)
    products = products * (weight[0] * (-0.5 / cells))
    both = jnp.concatenate([jnp.sum(squares, axis=0, keepdims=True), jnp.sum(products, axis=0, keepdims=True)], axis=0)
    sums[...] = jnp.broadcast_to(both[None], sums.shape)
    for z in range(planes):
        for h in range(parts):
            give(z, h).wait()


def total_kernel(groups, cells, everyone, norm, energy):
    values = everyone[...]
    mine = iota(values.shape, 0) % groups == lax.axis_index("pair")
    first = iota(values.shape, 1) == 0
    squares = jnp.sum(jnp.where(first & mine, values, 0.0))
    norm[0] = jnp.sqrt(jnp.full((1, 1), squares * (1.0 / cells), F32))[0, 0]
    energy[0] = jnp.sum(jnp.where(first, 0.0, values))


def exchange(value, pairs):
    return lax.ppermute(value, "gz", [move for a, b in pairs for move in ((a, b), (b, a))])


def params(mib):
    return pltpu.CompilerParams(vmem_limit_bytes=mib << 20)


def per_device(orbitals, pair_index, pair_weight):
    size = lax.axis_size("gz")
    groups = lax.axis_size("pair")
    _, planes, rows, columns = orbitals.shape
    parts = columns // LANES
    assert planes == 8 and columns == 2 * LANES and rows % (4 * ROWS) == 0 and pair_index.shape[0] == 1 and size % 2 == 0
    half = planes // 2
    mid_rows, low_rows = rows // 2, rows // 4
    tall, mid_tall, low_tall = rows + 2 * PAD, mid_rows + 2 * PAD, low_rows + 2 * PAD
    inner = [(i, i + 1) for i in range(0, size, 2)]
    outer = [(i, i + 1) for i in range(1, size - 1, 2)]

    def shape(*dims):
        return jax.ShapeDtypeStruct(dims, F32)

    def scratch(*dims):
        return pltpu.VMEM(dims, F32)

    three = (half + 2) // 2
    own_a, own_b, coarse_a, coarse_b = pl.pallas_call(
        functools.partial(fine_kernel, size),
        out_shape=[shape(half, parts, rows, LANES)] * 2 + [shape(three, mid_rows, LANES)] * 2,
        in_specs=[HBM, SMEM],
        out_specs=[ANY, ANY, VMEM, VMEM],
        scratch_shapes=[
            pltpu.VMEM((planes, rows, columns), orbitals.dtype),
            pltpu.VMEM((planes, rows, columns), orbitals.dtype),
            scratch(planes + 2, parts, tall, LANES),
            scratch(planes + 4, parts, tall, LANES),
            scratch(half + 2, mid_rows, LANES),
            pltpu.SemaphoreType.DMA((2, planes)),
            pltpu.SemaphoreType.DMA((2,)),
        ],
        compiler_params=params(58),
        name="fine",
    )(orbitals, pair_index.reshape(2))

    coarse_got_a = exchange(coarse_a, inner)
    coarse_got_b = exchange(coarse_b, outer)

    whole, next_a, next_b, packed = pl.pallas_call(
        functools.partial(middle_kernel, size),
        out_shape=[shape(half + 4, mid_rows, LANES)] + [shape(3, mid_rows, LANES)] * 2 + [shape(low_rows, LANES)],
        in_specs=[VMEM] * 4,
        out_specs=[VMEM] * 4,
        scratch_shapes=[scratch(half + 4, 1, mid_tall, LANES)] * 2,
        compiler_params=params(8),
        name="middle",
    )(coarse_a, coarse_b, coarse_got_a, coarse_got_b)

    partners = list(range(0, size, 2))
    arrived = [packed]
    for k in partners[1:]:
        arrived.append(exchange(packed, [(i, i ^ k) for i in range(size) if i < i ^ k]))
    next_got_a = exchange(next_a, inner)
    next_got_b = exchange(next_b, outer)
    own_got_a = exchange(own_a, inner)
    own_got_b = exchange(own_b, outer)
    arrived += [exchange(value, inner) for value in arrived]
    partners += [k ^ 1 for k in partners]

    correction = pl.pallas_call(
        functools.partial(low_kernel, size, tuple(partners)),
        out_shape=shape(half + 4, mid_rows, LANES),
        in_specs=[ANY] * (3 + len(partners)),
        out_specs=VMEM,
        scratch_shapes=[
            scratch(half + 10, 1, mid_tall, LANES),
            scratch(half + 8, 1, mid_tall, LANES),
            scratch(half + 6, 1, mid_tall, LANES),
            scratch(mid_rows, LANES),
            scratch(6, 1, mid_rows, LANES),
            scratch(size + 2, low_tall, LANES),
            scratch(size + 2, low_tall, LANES),
            scratch(size + 2, low_tall, LANES),
            scratch(size + 2, low_tall, LANES),
            scratch(3, size + 2, low_rows // 2 + 2 * PAD, LANES),
            scratch(size + 2, low_rows, LANES),
            pltpu.SemaphoreType.DMA((len(partners),)),
            pltpu.SemaphoreType.DMA((3,)),
        ],
        compiler_params=params(12),
        name="low",
    )(whole, next_got_a, next_got_b, *arrived)

    cells = planes * size * rows * columns
    potential, sums = pl.pallas_call(
        functools.partial(top_kernel, size, cells),
        out_shape=[shape(1, planes, rows, columns), shape(size * groups, 2, LANES)],
        in_specs=[ANY] * 4 + [VMEM, SMEM],
        out_specs=[ANY, VMEM],
        scratch_shapes=[
            scratch(planes + 8, parts, tall, LANES),
            scratch(planes + 6, parts, tall, LANES),
            scratch(planes + 4, parts, tall, LANES),
            scratch(planes + 2, parts, tall, LANES),
            scratch(half + 4, parts, rows, LANES),
            pltpu.SemaphoreType.DMA((4,)),
            pltpu.SemaphoreType.DMA((planes, parts)),
        ],
        compiler_params=params(24),
        name="top",
    )(own_a, own_b, own_got_a, own_got_b, correction, pair_weight)

    everyone = lax.all_to_all(sums, ("gz", "pair"), 0, 0)
    norm, energy = pl.pallas_call(
        functools.partial(total_kernel, groups, cells),
        out_shape=[shape(1)] * 2,
        in_specs=[VMEM],
        out_specs=[SMEM] * 2,
        name="total",
    )(everyone)
    return (potential, norm, energy)


def solution(mesh):
    return jax.shard_map(
        per_device,
        mesh=mesh,
        in_specs=(P(None, "gz", None, None), P("pair", None), P("pair")),
        out_specs=(P("pair", "gz", None, None), P("pair"), P()),
        check_vma=False,
    )
```

```python
import functools

import jax
import jax.numpy as jnp
from jax import lax
from jax.experimental import pallas as pl
from jax.experimental.pallas import tpu as pltpu
from jax.sharding import PartitionSpec as P


LANES = 128
PAD = 8
SWEEPS = 8
ROWS = 32
THIRD = 1.0 / 3.0
NINTH = 1.0 / 9.0
F32 = jnp.float32
BF16 = jnp.bfloat16
ANY = pl.BlockSpec(memory_space=pl.ANY)
VMEM = pl.BlockSpec(memory_space=pltpu.VMEM)
SMEM = pl.BlockSpec(memory_space=pltpu.SMEM)
HBM = pl.BlockSpec(memory_space=pltpu.HBM)


def scale(level):
    return 4.0**level / 9.0


def iota(shape, dim):
    return lax.broadcasted_iota(jnp.int32, shape, dim)


def split_dot(value, matrix):
    high = value.astype(BF16)
    low = (value - high.astype(F32)).astype(BF16)
    return jnp.dot(high, matrix, preferred_element_type=F32) + jnp.dot(low, matrix, preferred_element_type=F32)


def to_bf16(mask, value=1.0):
    return jnp.where(mask, value, 0.0).astype(BF16)


def neighbours(ref, z, row, rows):
    parts = ref.shape[1]
    here = pl.ds(PAD + row, rows)
    centre = [ref[z, h, here, :] for h in range(parts)]
    lane = iota((rows, LANES), 1)
    after = jnp.where(lane == 0, 0.0, pltpu.roll(centre[-1], 1, 1))
    before = jnp.where(lane == LANES - 1, 0.0, pltpu.roll(centre[0], LANES - 1, 1))
    sums = []
    for h in range(parts):
        total = ref[z, h, pl.ds(PAD + row - 1, rows), :] + ref[z, h, pl.ds(PAD + row + 1, rows), :]
        total += ref[z - 1, h, here, :] + ref[z + 1, h, here, :]
        total += centre[h - 1] if h else after
        total += centre[h + 1] if h + 1 < parts else before
        sums.append(total)
    return centre, sums


def zero_pads(ref, rows):
    blank = jnp.zeros((PAD, LANES), F32)

    def plane(z, _):
        for h in range(ref.shape[1]):
            ref[z, h, pl.ds(0, PAD), :] = blank
            ref[z, h, pl.ds(PAD + rows, PAD), :] = blank
        return 0

    lax.fori_loop(0, ref.shape[0], plane, 0)


def zero_planes(ref, planes, rows):
    for z in planes:
        for h in range(ref.shape[1]):
            ref[z, h, pl.ds(PAD, rows), :] = jnp.zeros((rows, LANES), F32)


def apply_planes(dst, src, first, last, shift, rows):
    def plane(z, _):
        for row in range(0, rows, ROWS):
            centre, sums = neighbours(src, z, row, ROWS)
            for h in range(len(centre)):
                dst[z + shift, h, pl.ds(PAD + row, ROWS), :] = (centre[h] * 3.0 + sums[h]) * NINTH
        return 0

    lax.fori_loop(first, last, plane, 0)


def paired_rows(ref, z, rows, offset):
    return [ref[z, h, pl.ds(PAD + offset, rows // 2, stride=2), :] for h in range(ref.shape[1])]


def restrict_columns(inner, far):
    lane = iota(far.shape, 1)
    pair = [a + b for a, b in zip(inner[1], inner[2])]
    outer = far + (inner[0][0] + inner[3][0]) + (inner[0][1] + inner[3][1])
    outer += jnp.where(lane == 0, 0.0, pltpu.roll(pair[1], 1, 1))
    outer += jnp.where(lane == LANES - 1, 0.0, pltpu.roll(pair[0], LANES - 1, 1))
    return ((pair[0] + pair[1]) * 6.0 + outer) * (NINTH / 8.0)


def total_of(*lists):
    return functools.reduce(lambda a, b: a + b, [v for values in lists for v in values])


def restrict_fine(ref, z, rows):
    inner = [[a + b for a, b in zip(paired_rows(ref, z, rows, k), paired_rows(ref, z + 1, rows, k))] for k in (-1, 0, 1, 2)]
    far = total_of(*(paired_rows(ref, p, rows, k) for p in (z - 1, z + 2) for k in (0, 1)))
    return restrict_columns(inner, far)


def restrict_pair(ref, z, rows, matrices):
    half = rows // 2

    def at(plane, offset):
        return ref[plane, 0, pl.ds(PAD + offset, half, stride=2), :]

    inner = [at(z, k) + at(z + 1, k) for k in (-1, 0, 1, 2)]
    outer = inner[0] + inner[3] + (at(z - 1, 0) + at(z - 1, 1)) + (at(z + 2, 0) + at(z + 2, 1))
    total = split_dot(inner[1] + inner[2], matrices[0]) + split_dot(outer, matrices[1])
    return total * (NINTH / 8.0)


def restrict_matrices(out_shift):
    row, column = iota((LANES, LANES), 0), iota((LANES, LANES), 1) - out_shift
    inside = (column >= 0) & (column < LANES // 2)
    own = (row >> 1) == column
    beside = (row == 2 * column - 1) | (row == 2 * column + 2)
    stencil = jnp.where(inside & own, 6.0, jnp.where(inside & beside, 1.0, 0.0)).astype(BF16)
    return stencil, to_bf16(inside & own)


def deal(parts):
    n = parts * LANES
    row, column = iota((n, n), 0), iota((n, n), 1)
    return to_bf16(row == parts * (column & (LANES - 1)) + (column >> 7))


def fine_kernel(size, orbitals, pair_index, own_a, own_b, coarse_a, coarse_b, once, left, right, source, smooth, sums, in_sem, out_sem):
    planes, rows = left.shape[0], left.shape[1]
    parts = source.shape[1]
    half = planes // 2
    me = lax.axis_index("gz")
    odd = me % 2

    def fetch(z):
        return [
            pltpu.make_async_copy(orbitals.at[pair_index[k], z], buffer.at[z], in_sem.at[k, z])
            for k, buffer in ((0, left), (1, right))
        ]

    for z in range(planes):
        for copy in fetch(z):
            copy.start()
    zero_pads(source, rows)
    zero_pads(smooth, rows)
    zero_planes(source, (0, planes + 1), rows)
    zero_planes(smooth, (0, 1, planes + 2, planes + 3), rows)
    dealt = deal(parts)

    def multiply(z, _):
        for copy in fetch(z):
            copy.wait()
        product = jnp.dot(left[z], dealt, preferred_element_type=F32) * jnp.dot(right[z], dealt, preferred_element_type=F32)
        for h in range(parts):
            source[z + 1, h, pl.ds(PAD, rows), :] = product[:, h * LANES : (h + 1) * LANES]
        return 0

    lax.fori_loop(0, planes, multiply, 0)

    def keep(start, target, k):
        return pltpu.make_async_copy(source.at[pl.ds(start, half), :, pl.ds(PAD, rows), :], target, out_sem.at[k])

    kept = [keep(1 + half * (1 - odd), own_a, 0), keep(1 + half * odd, own_b, 1)]

    apply_planes(smooth, source, 1, planes + 1, 1, rows)

    def spread(target, origin):
        for h in range(parts):
            smooth[target, h, pl.ds(PAD, rows), :] = source[origin, h, pl.ds(PAD, rows), :] * NINTH

    @pl.when(me > 0)
    def _():
        spread(1, 1)

    @pl.when(me < size - 1)
    def _():
        spread(planes + 2, planes)

    for copy in kept:
        copy.start()

    kept.append(pltpu.make_async_copy(smooth.at[pl.ds(2, planes), :, pl.ds(PAD, rows), :], once, out_sem.at[2]))
    kept[-1].start()

    def coarse(q, _):
        sums[q + 1] = restrict_fine(smooth, 2 * q + 2, rows)
        return 0

    lax.fori_loop(0, half, coarse, 0)

    def edge(plane, far):
        inner = [paired_rows(smooth, plane, rows, k) for k in (-1, 0, 1, 2)]
        return restrict_columns(inner, total_of(*(paired_rows(smooth, far, rows, k) for k in (0, 1))))

    sums[0] = jnp.where(me > 0, edge(1, 2), 0.0)
    sums[half + 1] = jnp.where(me < size - 1, edge(planes + 2, planes + 1), 0.0)

    three = (half + 2) // 2

    @pl.when(odd == 0)
    def _():
        coarse_a[...] = sums[pl.ds(three, three)]
        coarse_b[...] = sums[pl.ds(0, three)]

    @pl.when(odd == 1)
    def _():
        coarse_a[...] = sums[pl.ds(0, three)]
        coarse_b[...] = sums[pl.ds(three, three)]

    for copy in kept:
        copy.wait()


def middle_kernel(size, sent_a, sent_b, got_a, got_b, whole, next_a, next_b, packed, field, smooth):
    rows = sent_a.shape[1]
    planes = whole.shape[0] - 4
    me = lax.axis_index("gz")
    zero_pads(field, rows)
    zero_pads(smooth, rows)
    first, second = restrict_matrices(0), restrict_matrices(LANES // 2)

    def gather(own, low, high):
        centre = pl.ds(PAD, rows)
        n = planes
        for plane in range(n + 4):
            value = None
            if 1 <= plane <= n + 2:
                source, at = own[(plane - 1) // ((n + 2) // 2)], (plane - 1) % ((n + 2) // 2)
                value = source[at]
            if plane < 3:
                value = low[plane] if value is None else value + low[plane]
            if plane > n:
                value = high[plane - n - 1] if value is None else value + high[plane - n - 1]
            whole[plane] = value
            field[plane, 0, centre, :] = value

    @pl.when(me % 2 == 0)
    def _():
        gather((sent_b, sent_a), got_b, got_a)

    @pl.when(me % 2 == 1)
    def _():
        gather((sent_a, sent_b), got_a, got_b)

    apply_planes(smooth, field, jnp.where(me == 0, 2, 1), jnp.where(me == size - 1, planes + 2, planes + 3), 0, rows)

    @pl.when(me == 0)
    def _():
        zero_planes(smooth, (1,), rows)

    @pl.when(me == size - 1)
    def _():
        zero_planes(smooth, (planes + 2,), rows)

    packed[...] = restrict_pair(smooth, 2, rows, first) + restrict_pair(smooth, 4, rows, second)

    up, down = whole[pl.ds(1, 3)], whole[pl.ds(planes, 3)]

    @pl.when(me % 2 == 0)
    def _():
        next_a[...] = up
        next_b[...] = down

    @pl.when(me % 2 == 1)
    def _():
        next_a[...] = down
        next_b[...] = up


def packed_apply(ref, block, rows):
    centre = ref[block, pl.ds(PAD, rows), :]
    lane = iota((rows, LANES), 1)
    half = LANES // 2
    total = ref[block, pl.ds(PAD - 1, rows), :] + ref[block, pl.ds(PAD + 1, rows), :]
    other = jnp.where(lane >= half, ref[block - 1, pl.ds(PAD, rows), :], ref[block + 1, pl.ds(PAD, rows), :])
    total += pltpu.roll(centre + other, half, 1)
    total += jnp.where((lane & (half - 1)) == 0, 0.0, pltpu.roll(centre, 1, 1))
    total += jnp.where((lane & (half - 1)) == half - 1, 0.0, pltpu.roll(centre, LANES - 1, 1))
    return centre * THIRD + total * NINTH


def last_apply(ref, plane, rows, width):
    centre = ref[plane, pl.ds(PAD, rows), :]
    lane = iota((rows, LANES), 1)
    total = ref[plane, pl.ds(PAD - 1, rows), :] + ref[plane, pl.ds(PAD + 1, rows), :]
    total += ref[plane - 1, pl.ds(PAD, rows), :] + ref[plane + 1, pl.ds(PAD, rows), :]
    total += pltpu.roll(centre, 1, 1) + pltpu.roll(centre, LANES - 1, 1)
    return jnp.where(lane < width, centre * THIRD + total * NINTH, 0.0)


def coarse_levels(size, source, result, blocks, smooth, bottom, spare):
    rows = source.shape[1] - 2 * PAD
    half = rows // 2
    width = LANES // 4
    c2, c3 = scale(2), scale(3)
    row, column = iota((LANES, LANES), 0), iota((LANES, LANES), 1)
    gather = to_bf16(((row & (LANES // 2 - 1)) >> 1) == column)
    scatter = to_bf16(((column & (LANES // 2 - 1)) >> 1) == row)
    centre = pl.ds(PAD, rows)
    inner = pl.ds(PAD, half)

    for b in range(1, size + 1):
        smooth[b, centre, :] = packed_apply(source, b, rows)
    for b in range(1, size + 1):
        spare[b] = packed_apply(smooth, b, rows)
    for b in range(1, size + 1):
        pairs = spare[b, pl.ds(0, half, stride=2), :] + spare[b, pl.ds(1, half, stride=2), :]
        value = split_dot(pairs, gather) * (c3 / 8.0)
        bottom[2, b, inner, :] = value
        bottom[0, b, inner, :] = value
    now = 0
    for _ in range(SWEEPS - 1):
        for b in range(1, size + 1):
            bottom[1 - now, b, inner, :] = last_apply(bottom.at[now], b, half, width) + bottom[2, b, inner, :]
        now = 1 - now
    for b in range(1, size + 1):
        value = split_dot(bottom[now, b, inner, :], scatter)
        spare[b, pl.ds(0, half, stride=2), :] = value
        spare[b, pl.ds(1, half, stride=2), :] = value
    for b in range(1, size + 1):
        source_b = source[b, centre, :] * c2
        blocks[b, centre, :] = source_b + smooth[b, centre, :] * c2 + spare[b]
    for b in range(1, size + 1):
        smooth[b, centre, :] = packed_apply(blocks, b, rows) + source[b, centre, :] * c2
    for b in range(1, size + 1):
        result[b, centre, :] = packed_apply(smooth, b, rows) + source[b, centre, :] * c2


def bring_all(pairs, sem):
    copies = [pltpu.make_async_copy(origin, target, sem.at[k]) for k, (origin, target) in enumerate(pairs)]
    for copy in copies:
        copy.start()
    return copies


def start_level(dst, src, grown, planes, shift, offset, level, rows):
    c = scale(level) * NINTH

    def plane(z, _):
        for r in range(0, rows, ROWS):
            centre, total = neighbours(src, z, r, ROWS)
            for h in range(len(centre)):
                value = (centre[h] * 12.0 + total[h]) * c
                dst[z + shift, h, pl.ds(PAD + r, ROWS), :] = value + grown[(z + offset) >> 1, pl.ds(r, ROWS), :]
        return 0

    lax.fori_loop(*planes, plane, 0)


def sweep_level(dst, src, source, planes, shift, offset, level, rows):
    ratio = scale(level) / NINTH

    def plane(z, _):
        for r in range(0, rows, ROWS):
            centre, total = neighbours(src, z, r, ROWS)
            for h in range(len(centre)):
                value = source[z + offset, h, pl.ds(PAD + r, ROWS), :]
                value = value if ratio == 1.0 else value * ratio
                dst[z + shift, h, pl.ds(PAD + r, ROWS), :] = (centre[h] * 3.0 + total[h] + value) * NINTH
        return 0

    lax.fori_loop(*planes, plane, 0)


def span(me, size, halo, inside, shift=0):
    low = jnp.where(me == 0, halo, 0)
    high = jnp.where(me == size - 1, halo + inside, 2 * halo + inside)
    return low + shift, high + shift


def blank_outside(ref, me, size, halo, inside, rows):
    @pl.when(me == 0)
    def _():
        zero_planes(ref, range(halo), rows)

    @pl.when(me == size - 1)
    def _():
        zero_planes(ref, range(halo + inside, 2 * halo + inside), rows)


def pack_kernel(*refs):
    for k, ref in enumerate(refs[:-1]):
        refs[-1][k] = ref[...]


def low_kernel(size, partners, whole, next_a, next_b, mine, other, result, *scratch):
    (mid, first, second, _, grown) = scratch[:5]
    (low_source, low_result, low_blocks, low_smooth, bottom, spare, low_sem, mid_sem) = scratch[5:]
    rows = whole.shape[1]
    planes = whole.shape[0] - 4
    low_rows = mine.shape[1]
    me = lax.axis_index("gz")
    odd = me % 2
    blank = jnp.zeros((PAD, LANES), F32)
    inner = pl.ds(PAD, low_rows)
    middle = pl.ds(PAD, rows)
    edge = 3

    blocks = [
        (ref.at[k], low_source.at[jnp.bitwise_xor(me, partner ^ far) + 1, inner])
        for far, ref in ((0, mine), (1, other))
        for k, partner in enumerate(partners)
    ]
    low_copies = bring_all(blocks, low_sem)
    top = edge + planes + 4
    mid_copies = bring_all(
        [
            (whole, mid.at[pl.ds(edge, planes + 4), 0, middle]),
            (next_a, mid.at[pl.ds(top * (1 - odd), edge), 0, middle]),
            (next_b, mid.at[pl.ds(top * odd, edge), 0, middle]),
        ],
        mid_sem,
    )

    for ref in (mid, first, second):
        zero_pads(ref, rows)
    for ref in (low_source, low_blocks, low_smooth):
        for b in range(size + 2):
            ref[b, pl.ds(0, PAD), :] = blank
            ref[b, pl.ds(PAD + low_rows, PAD), :] = blank
        for b in (0, size + 1):
            ref[b, inner, :] = jnp.zeros((low_rows, LANES), F32)
    for k in range(2):
        for b in range(size + 2):
            bottom[k, b, pl.ds(0, PAD), :] = blank
            bottom[k, b, pl.ds(PAD + low_rows // 2, PAD), :] = blank
        for b in (0, size + 1):
            bottom[k, b] = jnp.zeros(bottom.shape[2:], F32)
    for b in (0, size + 1):
        low_result[b, inner, :] = jnp.zeros((low_rows, LANES), F32)
    blank_outside(first, me, size, 4, planes, rows)
    blank_outside(second, me, size, 3, planes, rows)

    for copy in low_copies:
        copy.wait()
    coarse_levels(size, low_source, low_result, low_blocks, low_smooth, bottom, spare)

    row, column = iota((LANES, LANES), 0), iota((LANES, LANES), 1)
    for k in range(3):
        block = low_result[me + k, inner, :]
        for side in range(2):
            value = split_dot(block, to_bf16((column >> 1) + side * (LANES // 2) == row))
            grown[2 * k + side, pl.ds(0, low_rows, stride=2), :] = value
            grown[2 * k + side, pl.ds(1, low_rows, stride=2), :] = value

    for copy in mid_copies:
        copy.wait()
    start_level(first, mid, grown, span(me, size, 4, planes, 1), -1, -1, 1, rows)
    sweep_level(second, first, mid, span(me, size, 3, planes, 1), -1, 1, 1, rows)
    c1 = scale(1)

    def last(z, _):
        for r in range(0, rows, ROWS):
            centre, total = neighbours(second, z + 1, r, ROWS)
            value = centre[0] * THIRD + total[0] * NINTH
            result[z, pl.ds(r, ROWS), :] = value + mid[z + 3, 0, pl.ds(PAD + r, ROWS), :] * c1
        return 0

    lax.fori_loop(*span(me, size, 2, planes), last, 0)


def top_kernel(size, cells, own_a, own_b, got_a, got_b, once, correction, weight, potential, sums, *scratch):
    field, first, second, third, grown, plain, in_sem, out_sem = scratch
    half, parts, rows = own_a.shape[0], own_a.shape[1], own_a.shape[2]
    planes = 2 * half
    mid_rows = correction.shape[1]
    me = lax.axis_index("gz")
    odd = me % 2

    def into(plane):
        return field.at[pl.ds(plane, half), :, pl.ds(PAD, rows), :]

    copies = bring_all(
        [
            (own_a, into(half + half * (1 - odd))),
            (own_b, into(half + half * odd)),
            (got_a, into(3 * half * (1 - odd))),
            (got_b, into(3 * half * odd)),
        ],
        in_sem,
    )
    for ref in (field, first, second, third):
        zero_pads(ref, rows)
    blank_outside(first, me, size, 3, planes, rows)
    blank_outside(second, me, size, 2, planes, rows)
    blank_outside(third, me, size, 1, planes, rows)

    def widen(z, _):
        value = correction[z]
        grown[z, pl.ds(0, mid_rows, stride=2), :] = value
        grown[z, pl.ds(1, mid_rows, stride=2), :] = value
        return 0

    lax.fori_loop(*span(me, size, 2, half), widen, 0)

    for copy in copies:
        copy.wait()
    low, high = span(me, size, 3, planes, 1)
    start_level(first, field, grown, (low, 4), -1, 0, 0, rows)
    start_level(first, field, grown, (4 + planes, high), -1, 0, 0, rows)
    c0 = scale(0)

    def begin(z, beside=None):
        for r in range(0, rows, ROWS):
            spread = grown[(z + half) >> 1, pl.ds(r, ROWS), :]
            for h in range(parts):
                value = field[z + half, h, pl.ds(PAD + r, ROWS), :] + once[z, h, pl.ds(r, ROWS), :]
                if beside is not None:
                    value += field[beside, h, pl.ds(PAD + r, ROWS), :] * NINTH
                first[z + 3, h, pl.ds(PAD + r, ROWS), :] = value * c0 + spread
        return 0

    begin(0, half - 1)
    lax.fori_loop(1, planes - 1, lambda z, _: begin(z), 0)
    begin(planes - 1, half + planes)
    sweep_level(second, first, field, span(me, size, 2, planes, 1), -1, 1, 0, rows)
    sweep_level(third, second, field, span(me, size, 1, planes, 1), -1, 2, 0, rows)

    def give(z):
        return pltpu.make_async_copy(plain.at[z], potential.at[0, z], out_sem.at[z])

    row, column = iota((2 * parts * LANES, parts * LANES), 0), iota((2 * parts * LANES, parts * LANES), 1)
    in_order = to_bf16(column == parts * (row & (LANES - 1)) + ((row >> 7) & (parts - 1)))

    def final(z, totals):
        squares, products = totals
        here = pl.ds(PAD, rows)
        whole = [third[z + 1, h, here, :] for h in range(parts)]
        upper = [value.astype(BF16) for value in whole]
        lower = [(value - part.astype(F32)).astype(BF16) for value, part in zip(whole, upper)]
        plain[z] = jnp.dot(jnp.concatenate(upper + lower, axis=1), in_order, preferred_element_type=F32)
        give(z).start()
        for r in range(0, rows, ROWS):
            centre, total = neighbours(third, z + 1, r, ROWS)
            for h in range(parts):
                f = field[z + half, h, pl.ds(PAD + r, ROWS), :]
                remain = f - 6.0 * centre[h] + total[h]
                squares += jnp.sum((remain * remain).reshape(ROWS // 8, 8, LANES), axis=0)
                products += jnp.sum((f * centre[h]).reshape(ROWS // 8, 8, LANES), axis=0)
        return squares, products

    squares, products = lax.fori_loop(0, planes, final, (jnp.zeros((8, LANES), F32),) * 2)
    products = products * (weight[0] * (-0.5 / cells))
    both = jnp.concatenate([jnp.sum(squares, axis=0, keepdims=True), jnp.sum(products, axis=0, keepdims=True)], axis=0)
    sums[...] = jnp.broadcast_to(both[None], sums.shape)
    for z in range(planes):
        give(z).wait()


def total_kernel(groups, cells, everyone, norm, energy):
    values = everyone[...]
    mine = iota(values.shape, 0) % groups == lax.axis_index("pair")
    first = iota(values.shape, 1) == 0
    squares = jnp.sum(jnp.where(first & mine, values, 0.0))
    norm[0] = jnp.sqrt(jnp.full((1, 1), squares * (1.0 / cells), F32))[0, 0]
    energy[0] = jnp.sum(jnp.where(first, 0.0, values))


def exchange(value, pairs):
    return lax.ppermute(value, "gz", [move for a, b in pairs for move in ((a, b), (b, a))])


def params(mib):
    return pltpu.CompilerParams(vmem_limit_bytes=mib << 20)


def per_device(orbitals, pair_index, pair_weight):
    size = lax.axis_size("gz")
    groups = lax.axis_size("pair")
    _, planes, rows, columns = orbitals.shape
    parts = columns // LANES
    assert planes == 8 and columns == 2 * LANES and rows % (4 * ROWS) == 0 and pair_index.shape[0] == 1 and size % 2 == 0
    half = planes // 2
    mid_rows, low_rows = rows // 2, rows // 4
    tall, mid_tall, low_tall = rows + 2 * PAD, mid_rows + 2 * PAD, low_rows + 2 * PAD
    inner = [(i, i + 1) for i in range(0, size, 2)]
    outer = [(i, i + 1) for i in range(1, size - 1, 2)]

    def shape(*dims):
        return jax.ShapeDtypeStruct(dims, F32)

    def scratch(*dims):
        return pltpu.VMEM(dims, F32)

    three = (half + 2) // 2
    own_a, own_b, coarse_a, coarse_b, once = pl.pallas_call(
        functools.partial(fine_kernel, size),
        out_shape=[shape(half, parts, rows, LANES)] * 2 + [shape(three, mid_rows, LANES)] * 2 + [shape(planes, parts, rows, LANES)],
        in_specs=[HBM, SMEM],
        out_specs=[ANY, ANY, VMEM, VMEM, ANY],
        scratch_shapes=[
            pltpu.VMEM((planes, rows, columns), orbitals.dtype),
            pltpu.VMEM((planes, rows, columns), orbitals.dtype),
            scratch(planes + 2, parts, tall, LANES),
            scratch(planes + 4, parts, tall, LANES),
            scratch(half + 2, mid_rows, LANES),
            pltpu.SemaphoreType.DMA((2, planes)),
            pltpu.SemaphoreType.DMA((3,)),
        ],
        compiler_params=params(48),
        name="fine",
    )(orbitals, pair_index.reshape(2))

    coarse_got_a = exchange(coarse_a, inner)
    coarse_got_b = exchange(coarse_b, outer)

    whole, next_a, next_b, packed = pl.pallas_call(
        functools.partial(middle_kernel, size),
        out_shape=[shape(half + 4, mid_rows, LANES)] + [shape(3, mid_rows, LANES)] * 2 + [shape(low_rows, LANES)],
        in_specs=[VMEM] * 4,
        out_specs=[VMEM] * 4,
        scratch_shapes=[scratch(half + 4, 1, mid_tall, LANES)] * 2,
        compiler_params=params(8),
        name="middle",
    )(coarse_a, coarse_b, coarse_got_a, coarse_got_b)

    partners = list(range(0, size, 2))
    arrived = [packed]
    for k in partners[1:]:
        arrived.append(exchange(packed, [(i, i ^ k) for i in range(size) if i < i ^ k]))
    next_got_a = exchange(next_a, inner)
    next_got_b = exchange(next_b, outer)
    own_got_a = exchange(own_a, inner)
    own_got_b = exchange(own_b, outer)
    mine = pl.pallas_call(
        pack_kernel,
        out_shape=shape(len(partners), low_rows, LANES),
        in_specs=[VMEM] * len(partners),
        out_specs=VMEM,
        compiler_params=params(4),
        name="pack",
    )(*arrived)
    other = exchange(mine, inner)

    correction = pl.pallas_call(
        functools.partial(low_kernel, size, tuple(partners)),
        out_shape=shape(half + 4, mid_rows, LANES),
        in_specs=[ANY] * 5,
        out_specs=VMEM,
        scratch_shapes=[
            scratch(half + 10, 1, mid_tall, LANES),
            scratch(half + 8, 1, mid_tall, LANES),
            scratch(half + 6, 1, mid_tall, LANES),
            scratch(mid_rows, LANES),
            scratch(6, mid_rows, LANES),
            scratch(size + 2, low_tall, LANES),
            scratch(size + 2, low_tall, LANES),
            scratch(size + 2, low_tall, LANES),
            scratch(size + 2, low_tall, LANES),
            scratch(3, size + 2, low_rows // 2 + 2 * PAD, LANES),
            scratch(size + 2, low_rows, LANES),
            pltpu.SemaphoreType.DMA((2 * len(partners),)),
            pltpu.SemaphoreType.DMA((3,)),
        ],
        compiler_params=params(12),
        name="low",
    )(whole, next_got_a, next_got_b, mine, other)

    cells = planes * size * rows * columns
    potential, sums = pl.pallas_call(
        functools.partial(top_kernel, size, cells),
        out_shape=[shape(1, planes, rows, columns), shape(size * groups, 2, LANES)],
        in_specs=[ANY] * 4 + [VMEM, VMEM, SMEM],
        out_specs=[ANY, VMEM],
        scratch_shapes=[
            scratch(planes + 8, parts, tall, LANES),
            scratch(planes + 6, parts, tall, LANES),
            scratch(planes + 4, parts, tall, LANES),
            scratch(planes + 2, parts, tall, LANES),
            scratch(half + 4, rows, LANES),
            scratch(planes, rows, columns),
            pltpu.SemaphoreType.DMA((4,)),
            pltpu.SemaphoreType.DMA((planes,)),
        ],
        compiler_params=params(24),
        name="top",
    )(own_a, own_b, own_got_a, own_got_b, once, correction, pair_weight)

    everyone = lax.all_to_all(sums, ("gz", "pair"), 0, 0)
    norm, energy = pl.pallas_call(
        functools.partial(total_kernel, groups, cells),
        out_shape=[shape(1)] * 2,
        in_specs=[VMEM],
        out_specs=[SMEM] * 2,
        name="total",
    )(everyone)
    return (potential, norm, energy)


def solution(mesh):
    return jax.shard_map(
        per_device,
        mesh=mesh,
        in_specs=(P(None, "gz", None, None), P("pair", None), P("pair")),
        out_specs=(P("pair", "gz", None, None), P("pair"), P()),
        check_vma=False,
    )
```

```python
import functools

import jax
import jax.numpy as jnp
from jax import lax
from jax.experimental import pallas as pl
from jax.experimental.pallas import tpu as pltpu
from jax.sharding import PartitionSpec as P


LANES = 128
PAD = 8
SWEEPS = 8
ROWS = 32
THIRD = 1.0 / 3.0
NINTH = 1.0 / 9.0
F32 = jnp.float32
BF16 = jnp.bfloat16
ANY = pl.BlockSpec(memory_space=pl.ANY)
VMEM = pl.BlockSpec(memory_space=pltpu.VMEM)
SMEM = pl.BlockSpec(memory_space=pltpu.SMEM)
HBM = pl.BlockSpec(memory_space=pltpu.HBM)


def scale(level):
    return 4.0**level / 9.0


def iota(shape, dim):
    return lax.broadcasted_iota(jnp.int32, shape, dim)


def split_dot(value, matrix):
    high = value.astype(BF16)
    low = (value - high.astype(F32)).astype(BF16)
    return jnp.dot(high, matrix, preferred_element_type=F32) + jnp.dot(low, matrix, preferred_element_type=F32)


def to_bf16(mask, value=1.0):
    return jnp.where(mask, value, 0.0).astype(BF16)


def neighbours(ref, z, row, rows):
    parts = ref.shape[1]
    here = pl.ds(PAD + row, rows)
    centre = [ref[z, h, here, :] for h in range(parts)]
    lane = iota((rows, LANES), 1)
    after = jnp.where(lane == 0, 0.0, pltpu.roll(centre[-1], 1, 1))
    before = jnp.where(lane == LANES - 1, 0.0, pltpu.roll(centre[0], LANES - 1, 1))
    sums = []
    for h in range(parts):
        total = ref[z, h, pl.ds(PAD + row - 1, rows), :] + ref[z, h, pl.ds(PAD + row + 1, rows), :]
        total += ref[z - 1, h, here, :] + ref[z + 1, h, here, :]
        total += centre[h - 1] if h else after
        total += centre[h + 1] if h + 1 < parts else before
        sums.append(total)
    return centre, sums


def zero_pads(ref, rows):
    blank = jnp.zeros((PAD, LANES), F32)

    def plane(z, _):
        for h in range(ref.shape[1]):
            ref[z, h, pl.ds(0, PAD), :] = blank
            ref[z, h, pl.ds(PAD + rows, PAD), :] = blank
        return 0

    lax.fori_loop(0, ref.shape[0], plane, 0)


def zero_planes(ref, planes, rows):
    for z in planes:
        for h in range(ref.shape[1]):
            ref[z, h, pl.ds(PAD, rows), :] = jnp.zeros((rows, LANES), F32)


def apply_planes(dst, src, first, last, shift, rows):
    def plane(z):
        for row in range(0, rows, ROWS):
            centre, sums = neighbours(src, z, row, ROWS)
            for h in range(len(centre)):
                dst[z + shift, h, pl.ds(PAD + row, ROWS), :] = (centre[h] * 3.0 + sums[h]) * NINTH

    each_plane(first, last, plane)


def paired_rows(ref, z, rows, offset):
    return [ref[z, h, pl.ds(PAD + offset, rows // 2, stride=2), :] for h in range(ref.shape[1])]


def restrict_columns(inner, far):
    lane = iota(far.shape, 1)
    pair = [a + b for a, b in zip(inner[1], inner[2])]
    outer = far + (inner[0][0] + inner[3][0]) + (inner[0][1] + inner[3][1])
    outer += jnp.where(lane == 0, 0.0, pltpu.roll(pair[1], 1, 1))
    outer += jnp.where(lane == LANES - 1, 0.0, pltpu.roll(pair[0], LANES - 1, 1))
    return ((pair[0] + pair[1]) * 6.0 + outer) * (NINTH / 8.0)


def total_of(*lists):
    return functools.reduce(lambda a, b: a + b, [v for values in lists for v in values])


def restrict_fine(ref, z, rows):
    inner = [[a + b for a, b in zip(paired_rows(ref, z, rows, k), paired_rows(ref, z + 1, rows, k))] for k in (-1, 0, 1, 2)]
    far = total_of(*(paired_rows(ref, p, rows, k) for p in (z - 1, z + 2) for k in (0, 1)))
    return restrict_columns(inner, far)


def restrict_pair(ref, z, rows, matrices):
    half = rows // 2

    def at(plane, offset):
        return ref[plane, 0, pl.ds(PAD + offset, half, stride=2), :]

    inner = [at(z, k) + at(z + 1, k) for k in (-1, 0, 1, 2)]
    outer = inner[0] + inner[3] + (at(z - 1, 0) + at(z - 1, 1)) + (at(z + 2, 0) + at(z + 2, 1))
    total = split_dot(inner[1] + inner[2], matrices[0]) + split_dot(outer, matrices[1])
    return total * (NINTH / 8.0)


def restrict_matrices(out_shift):
    row, column = iota((LANES, LANES), 0), iota((LANES, LANES), 1) - out_shift
    inside = (column >= 0) & (column < LANES // 2)
    own = (row >> 1) == column
    beside = (row == 2 * column - 1) | (row == 2 * column + 2)
    stencil = jnp.where(inside & own, 6.0, jnp.where(inside & beside, 1.0, 0.0)).astype(BF16)
    return stencil, to_bf16(inside & own)


def deal(parts):
    n = parts * LANES
    row, column = iota((n, n), 0), iota((n, n), 1)
    return to_bf16(row == parts * (column & (LANES - 1)) + (column >> 7))


def fine_kernel(size, cuts, orbitals, pair_index, *refs):
    own, (coarse_a, coarse_b, once, left, right, source, smooth, sums, in_sem, out_sem) = refs[: 2 * len(cuts)], refs[2 * len(cuts) :]
    planes, rows = left.shape[0], left.shape[1]
    parts = source.shape[1]
    half = planes // 2
    me = lax.axis_index("gz")
    odd = me % 2

    def fetch(z):
        return [
            pltpu.make_async_copy(orbitals.at[pair_index[k], z], buffer.at[z], in_sem.at[k, z])
            for k, buffer in ((0, left), (1, right))
        ]

    for z in range(planes):
        for copy in fetch(z):
            copy.start()
    zero_pads(source, rows)
    zero_pads(smooth, rows)
    zero_planes(source, (0, planes + 1), rows)
    zero_planes(smooth, (0, 1, planes + 2, planes + 3), rows)
    dealt = deal(parts)

    def multiply(z, _):
        for copy in fetch(z):
            copy.wait()
        product = jnp.dot(left[z], dealt, preferred_element_type=F32) * jnp.dot(right[z], dealt, preferred_element_type=F32)
        for h in range(parts):
            source[z + 1, h, pl.ds(PAD, rows), :] = product[:, h * LANES : (h + 1) * LANES]
        return 0

    lax.fori_loop(0, planes, multiply, 0)

    def keep(start, target, k):
        return pltpu.make_async_copy(source.at[pl.ds(start, target.shape[0]), :, pl.ds(PAD, rows), :], target, out_sem.at[k])

    kept = []
    for k, cut in enumerate(cuts):
        kept.append(keep(1 + half * (1 - odd) + cut, own[2 * k], 2 * k))
        kept.append(keep(1 + half * odd + cut, own[2 * k + 1], 2 * k + 1))

    apply_planes(smooth, source, 1, planes + 1, 1, rows)

    def spread(target, origin):
        for h in range(parts):
            smooth[target, h, pl.ds(PAD, rows), :] = source[origin, h, pl.ds(PAD, rows), :] * NINTH

    @pl.when(me > 0)
    def _():
        spread(1, 1)

    @pl.when(me < size - 1)
    def _():
        spread(planes + 2, planes)

    for copy in kept:
        copy.start()

    kept.append(pltpu.make_async_copy(smooth.at[pl.ds(2, planes), :, pl.ds(PAD, rows), :], once, out_sem.at[2 * len(cuts)]))
    kept[-1].start()

    def coarse(q, _):
        sums[q + 1] = restrict_fine(smooth, 2 * q + 2, rows)
        return 0

    lax.fori_loop(0, half, coarse, 0)

    def edge(plane, far):
        inner = [paired_rows(smooth, plane, rows, k) for k in (-1, 0, 1, 2)]
        return restrict_columns(inner, total_of(*(paired_rows(smooth, far, rows, k) for k in (0, 1))))

    sums[0] = jnp.where(me > 0, edge(1, 2), 0.0)
    sums[half + 1] = jnp.where(me < size - 1, edge(planes + 2, planes + 1), 0.0)

    three = (half + 2) // 2

    @pl.when(odd == 0)
    def _():
        coarse_a[...] = sums[pl.ds(three, three)]
        coarse_b[...] = sums[pl.ds(0, three)]

    @pl.when(odd == 1)
    def _():
        coarse_a[...] = sums[pl.ds(0, three)]
        coarse_b[...] = sums[pl.ds(three, three)]

    for copy in kept:
        copy.wait()


def middle_kernel(size, sent_a, sent_b, got_a, got_b, whole, next_a, next_b, packed, field, smooth):
    rows = sent_a.shape[1]
    planes = whole.shape[0] - 4
    me = lax.axis_index("gz")
    zero_pads(field, rows)
    zero_pads(smooth, rows)
    first, second = restrict_matrices(0), restrict_matrices(LANES // 2)

    def gather(own, low, high):
        centre = pl.ds(PAD, rows)
        n = planes
        for plane in range(n + 4):
            value = None
            if 1 <= plane <= n + 2:
                source, at = own[(plane - 1) // ((n + 2) // 2)], (plane - 1) % ((n + 2) // 2)
                value = source[at]
            if plane < 3:
                value = low[plane] if value is None else value + low[plane]
            if plane > n:
                value = high[plane - n - 1] if value is None else value + high[plane - n - 1]
            whole[plane] = value
            field[plane, 0, centre, :] = value

    @pl.when(me % 2 == 0)
    def _():
        gather((sent_b, sent_a), got_b, got_a)

    @pl.when(me % 2 == 1)
    def _():
        gather((sent_a, sent_b), got_a, got_b)

    apply_planes(smooth, field, 1, planes + 3, 0, rows)

    @pl.when(me == 0)
    def _():
        zero_planes(smooth, (1,), rows)

    @pl.when(me == size - 1)
    def _():
        zero_planes(smooth, (planes + 2,), rows)

    packed[...] = restrict_pair(smooth, 2, rows, first) + restrict_pair(smooth, 4, rows, second)

    up, down = whole[pl.ds(1, 3)], whole[pl.ds(planes, 3)]

    @pl.when(me % 2 == 0)
    def _():
        next_a[...] = up
        next_b[...] = down

    @pl.when(me % 2 == 1)
    def _():
        next_a[...] = down
        next_b[...] = up


def packed_apply(ref, block, rows):
    centre = ref[block, pl.ds(PAD, rows), :]
    lane = iota((rows, LANES), 1)
    half = LANES // 2
    total = ref[block, pl.ds(PAD - 1, rows), :] + ref[block, pl.ds(PAD + 1, rows), :]
    other = jnp.where(lane >= half, ref[block - 1, pl.ds(PAD, rows), :], ref[block + 1, pl.ds(PAD, rows), :])
    total += pltpu.roll(centre + other, half, 1)
    total += jnp.where((lane & (half - 1)) == 0, 0.0, pltpu.roll(centre, 1, 1))
    total += jnp.where((lane & (half - 1)) == half - 1, 0.0, pltpu.roll(centre, LANES - 1, 1))
    return centre * THIRD + total * NINTH


def last_apply(ref, plane, rows, width):
    centre = ref[plane, pl.ds(PAD, rows), :]
    lane = iota((rows, LANES), 1)
    total = ref[plane, pl.ds(PAD - 1, rows), :] + ref[plane, pl.ds(PAD + 1, rows), :]
    total += ref[plane - 1, pl.ds(PAD, rows), :] + ref[plane + 1, pl.ds(PAD, rows), :]
    total += pltpu.roll(centre, 1, 1) + pltpu.roll(centre, LANES - 1, 1)
    return jnp.where(lane < width, centre * THIRD + total * NINTH, 0.0)


def coarse_levels(size, source, result, blocks, smooth, bottom, spare):
    rows = source.shape[1] - 2 * PAD
    half = rows // 2
    width = LANES // 4
    c2, c3 = scale(2), scale(3)
    row, column = iota((LANES, LANES), 0), iota((LANES, LANES), 1)
    gather = to_bf16(((row & (LANES // 2 - 1)) >> 1) == column)
    scatter = to_bf16(((column & (LANES // 2 - 1)) >> 1) == row)
    centre = pl.ds(PAD, rows)
    inner = pl.ds(PAD, half)

    for b in range(1, size + 1):
        smooth[b, centre, :] = packed_apply(source, b, rows)
    for b in range(1, size + 1):
        spare[b] = packed_apply(smooth, b, rows)
    for b in range(1, size + 1):
        pairs = spare[b, pl.ds(0, half, stride=2), :] + spare[b, pl.ds(1, half, stride=2), :]
        value = split_dot(pairs, gather) * (c3 / 8.0)
        bottom[2, b, inner, :] = value
        bottom[0, b, inner, :] = value
    now = 0
    for _ in range(SWEEPS - 1):
        for b in range(1, size + 1):
            bottom[1 - now, b, inner, :] = last_apply(bottom.at[now], b, half, width) + bottom[2, b, inner, :]
        now = 1 - now
    for b in range(1, size + 1):
        value = split_dot(bottom[now, b, inner, :], scatter)
        spare[b, pl.ds(0, half, stride=2), :] = value
        spare[b, pl.ds(1, half, stride=2), :] = value
    for b in range(1, size + 1):
        source_b = source[b, centre, :] * c2
        blocks[b, centre, :] = source_b + smooth[b, centre, :] * c2 + spare[b]
    for b in range(1, size + 1):
        smooth[b, centre, :] = packed_apply(blocks, b, rows) + source[b, centre, :] * c2
    for b in range(1, size + 1):
        result[b, centre, :] = packed_apply(smooth, b, rows) + source[b, centre, :] * c2


def each_plane(first, last, body, step=2):
    def several(k, _):
        for i in range(step):
            body(first + step * k + i)
        return 0

    lax.fori_loop(0, (last - first) // step, several, 0)
    for z in range(last - (last - first) % step, last):
        body(z)


def bring_all(pairs, sem):
    copies = [pltpu.make_async_copy(origin, target, sem.at[k]) for k, (origin, target) in enumerate(pairs)]
    for copy in copies:
        copy.start()
    return copies


def start_level(dst, src, grown, planes, shift, offset, level, rows):
    c = scale(level) * NINTH

    def plane(z):
        for r in range(0, rows, ROWS):
            centre, total = neighbours(src, z, r, ROWS)
            for h in range(len(centre)):
                value = (centre[h] * 12.0 + total[h]) * c
                dst[z + shift, h, pl.ds(PAD + r, ROWS), :] = value + grown[(z + offset) >> 1, pl.ds(r, ROWS), :]

    each_plane(*planes, plane)


def sweep_level(dst, src, source, planes, shift, offset, level, rows):
    ratio = scale(level) / NINTH

    def plane(z):
        for r in range(0, rows, ROWS):
            centre, total = neighbours(src, z, r, ROWS)
            for h in range(len(centre)):
                value = source[z + offset, h, pl.ds(PAD + r, ROWS), :]
                value = value if ratio == 1.0 else value * ratio
                dst[z + shift, h, pl.ds(PAD + r, ROWS), :] = (centre[h] * 3.0 + total[h] + value) * NINTH

    each_plane(*planes, plane)


def blank_outside(ref, me, size, halo, inside, rows):
    @pl.when(me == 0)
    def _():
        zero_planes(ref, range(halo), rows)

    @pl.when(me == size - 1)
    def _():
        zero_planes(ref, range(halo + inside, 2 * halo + inside), rows)


def pack_kernel(*refs):
    for k, ref in enumerate(refs[:-1]):
        refs[-1][k] = ref[...]


def low_kernel(size, partners, whole, next_a, next_b, mine, other, result, *scratch):
    (mid, first, second, _, grown) = scratch[:5]
    (low_source, low_result, low_blocks, low_smooth, bottom, spare, low_sem, mid_sem) = scratch[5:]
    rows = whole.shape[1]
    planes = whole.shape[0] - 4
    low_rows = mine.shape[1]
    me = lax.axis_index("gz")
    odd = me % 2
    blank = jnp.zeros((PAD, LANES), F32)
    inner = pl.ds(PAD, low_rows)
    middle = pl.ds(PAD, rows)
    edge = 3

    blocks = [
        (ref.at[k], low_source.at[jnp.bitwise_xor(me, partner ^ far) + 1, inner])
        for far, ref in ((0, mine), (1, other))
        for k, partner in enumerate(partners)
    ]
    low_copies = bring_all(blocks, low_sem)
    top = edge + planes + 4
    mid_copies = bring_all(
        [
            (whole, mid.at[pl.ds(edge, planes + 4), 0, middle]),
            (next_a, mid.at[pl.ds(top * (1 - odd), edge), 0, middle]),
            (next_b, mid.at[pl.ds(top * odd, edge), 0, middle]),
        ],
        mid_sem,
    )

    for ref in (mid, first, second):
        zero_pads(ref, rows)
    for ref in (low_source, low_blocks, low_smooth):
        for b in range(size + 2):
            ref[b, pl.ds(0, PAD), :] = blank
            ref[b, pl.ds(PAD + low_rows, PAD), :] = blank
        for b in (0, size + 1):
            ref[b, inner, :] = jnp.zeros((low_rows, LANES), F32)
    for k in range(2):
        for b in range(size + 2):
            bottom[k, b, pl.ds(0, PAD), :] = blank
            bottom[k, b, pl.ds(PAD + low_rows // 2, PAD), :] = blank
        for b in (0, size + 1):
            bottom[k, b] = jnp.zeros(bottom.shape[2:], F32)
    for b in (0, size + 1):
        low_result[b, inner, :] = jnp.zeros((low_rows, LANES), F32)
    for copy in low_copies:
        copy.wait()
    coarse_levels(size, low_source, low_result, low_blocks, low_smooth, bottom, spare)

    row, column = iota((LANES, LANES), 0), iota((LANES, LANES), 1)
    for k in range(3):
        block = low_result[me + k, inner, :]
        for side in range(2):
            value = split_dot(block, to_bf16((column >> 1) + side * (LANES // 2) == row))
            grown[2 * k + side, pl.ds(0, low_rows, stride=2), :] = value
            grown[2 * k + side, pl.ds(1, low_rows, stride=2), :] = value

    for copy in mid_copies:
        copy.wait()
    start_level(first, mid, grown, (1, planes + 9), -1, -1, 1, rows)
    blank_outside(first, me, size, 4, planes, rows)
    sweep_level(second, first, mid, (1, planes + 7), -1, 1, 1, rows)
    blank_outside(second, me, size, 3, planes, rows)
    ratio = scale(1) / NINTH

    def last(z):
        for r in range(0, rows, ROWS):
            centre, total = neighbours(second, z + 1, r, ROWS)
            value = mid[z + 3, 0, pl.ds(PAD + r, ROWS), :] * ratio
            result[z, pl.ds(r, ROWS), :] = (centre[0] * 3.0 + total[0] + value) * NINTH

    each_plane(0, planes + 4, last)


def top_kernel(size, cells, cuts, *refs):
    own, got = refs[: 2 * len(cuts)], refs[2 * len(cuts) : 4 * len(cuts)]
    once, correction, weight, potential, sums, *scratch = refs[4 * len(cuts) :]
    field, first, second, third, grown, plain, in_sem, out_sem = scratch
    planes, parts, rows = once.shape[0], once.shape[1], once.shape[2]
    half = planes // 2
    mid_rows = correction.shape[1]
    me = lax.axis_index("gz")
    odd = me % 2

    def into(origin, plane):
        return origin, field.at[pl.ds(plane, origin.shape[0]), :, pl.ds(PAD, rows), :]

    moves = []
    for k, cut in enumerate(cuts):
        moves += [
            into(own[2 * k], half + half * (1 - odd) + cut),
            into(own[2 * k + 1], half + half * odd + cut),
            into(got[2 * k], 3 * half * (1 - odd) + cut),
            into(got[2 * k + 1], 3 * half * odd + cut),
        ]
    copies = bring_all(moves, in_sem)
    for ref in (field, first, second, third):
        zero_pads(ref, rows)

    def widen(z):
        value = correction[z]
        grown[z, pl.ds(0, mid_rows, stride=2), :] = value
        grown[z, pl.ds(1, mid_rows, stride=2), :] = value

    each_plane(0, half + 4, widen)

    for copy in copies:
        copy.wait()
    start_level(first, field, grown, (1, half), -1, 0, 0, rows)
    start_level(first, field, grown, (half + planes, 2 * half + planes - 1), -1, 0, 0, rows)
    c0 = scale(0)

    def begin(z, beside=None):
        for r in range(0, rows, ROWS):
            spread = grown[(z + half) >> 1, pl.ds(r, ROWS), :]
            for h in range(parts):
                value = field[z + half, h, pl.ds(PAD + r, ROWS), :] + once[z, h, pl.ds(r, ROWS), :]
                if beside is not None:
                    value += field[beside, h, pl.ds(PAD + r, ROWS), :] * NINTH
                first[z + 3, h, pl.ds(PAD + r, ROWS), :] = value * c0 + spread

    begin(0, half - 1)
    each_plane(1, planes - 1, begin)
    begin(planes - 1, half + planes)
    blank_outside(first, me, size, 3, planes, rows)
    sweep_level(second, first, field, (1, planes + 5), -1, 1, 0, rows)
    blank_outside(second, me, size, 2, planes, rows)
    sweep_level(third, second, field, (1, planes + 3), -1, 2, 0, rows)
    blank_outside(third, me, size, 1, planes, rows)

    def give(z):
        return pltpu.make_async_copy(plain.at[z], potential.at[0, z], out_sem.at[z])

    row, column = iota((2 * parts * LANES, parts * LANES), 0), iota((2 * parts * LANES, parts * LANES), 1)
    in_order = to_bf16(column == parts * (row & (LANES - 1)) + ((row >> 7) & (parts - 1)))

    def final(z, totals):
        squares, products = totals
        here = pl.ds(PAD, rows)
        whole = [third[z + 1, h, here, :] for h in range(parts)]
        upper = [value.astype(BF16) for value in whole]
        lower = [(value - part.astype(F32)).astype(BF16) for value, part in zip(whole, upper)]
        plain[z] = jnp.dot(jnp.concatenate(upper + lower, axis=1), in_order, preferred_element_type=F32)
        give(z).start()
        for r in range(0, rows, ROWS):
            centre, total = neighbours(third, z + 1, r, ROWS)
            for h in range(parts):
                f = field[z + half, h, pl.ds(PAD + r, ROWS), :]
                remain = f - 6.0 * centre[h] + total[h]
                squares += jnp.sum((remain * remain).reshape(ROWS // 8, 8, LANES), axis=0)
                products += jnp.sum((f * centre[h]).reshape(ROWS // 8, 8, LANES), axis=0)
        return squares, products

    squares, products = lax.fori_loop(0, planes, final, (jnp.zeros((8, LANES), F32),) * 2)
    products = products * (weight[0] * (-0.5 / cells))
    both = jnp.concatenate([jnp.sum(squares, axis=0, keepdims=True), jnp.sum(products, axis=0, keepdims=True)], axis=0)
    sums[...] = jnp.broadcast_to(both[None], sums.shape)
    for z in range(planes):
        give(z).wait()


def total_kernel(groups, cells, everyone, norm, energy):
    values = everyone[...]
    mine = iota(values.shape, 0) % groups == lax.axis_index("pair")
    first = iota(values.shape, 1) == 0
    squares = jnp.sum(jnp.where(first & mine, values, 0.0))
    norm[0] = jnp.sqrt(jnp.full((1, 1), squares * (1.0 / cells), F32))[0, 0]
    energy[0] = jnp.sum(jnp.where(first, 0.0, values))


def exchange(value, pairs):
    return lax.ppermute(value, "gz", [move for a, b in pairs for move in ((a, b), (b, a))])


def params(mib):
    return pltpu.CompilerParams(vmem_limit_bytes=mib << 20)


def per_device(orbitals, pair_index, pair_weight):
    size = lax.axis_size("gz")
    groups = lax.axis_size("pair")
    _, planes, rows, columns = orbitals.shape
    parts = columns // LANES
    assert planes == 8 and columns == 2 * LANES and rows % (4 * ROWS) == 0 and pair_index.shape[0] == 1 and size % 2 == 0
    half = planes // 2
    mid_rows, low_rows = rows // 2, rows // 4
    tall, mid_tall, low_tall = rows + 2 * PAD, mid_rows + 2 * PAD, low_rows + 2 * PAD
    inner = [(i, i + 1) for i in range(0, size, 2)]
    outer = [(i, i + 1) for i in range(1, size - 1, 2)]

    def shape(*dims):
        return jax.ShapeDtypeStruct(dims, F32)

    def scratch(*dims):
        return pltpu.VMEM(dims, F32)

    three = (half + 2) // 2
    counts = (half - half // 2, half // 2)
    cuts = (0, counts[0])
    own_shapes = [shape(count, parts, rows, LANES) for count in counts for _ in range(2)]
    *own, coarse_a, coarse_b, once = pl.pallas_call(
        functools.partial(fine_kernel, size, cuts),
        out_shape=own_shapes + [shape(three, mid_rows, LANES)] * 2 + [shape(planes, parts, rows, LANES)],
        in_specs=[HBM, SMEM],
        out_specs=[ANY] * len(own_shapes) + [VMEM, VMEM, ANY],
        scratch_shapes=[
            pltpu.VMEM((planes, rows, columns), orbitals.dtype),
            pltpu.VMEM((planes, rows, columns), orbitals.dtype),
            scratch(planes + 2, parts, tall, LANES),
            scratch(planes + 4, parts, tall, LANES),
            scratch(half + 2, mid_rows, LANES),
            pltpu.SemaphoreType.DMA((2, planes)),
            pltpu.SemaphoreType.DMA((len(own_shapes) + 1,)),
        ],
        compiler_params=params(48),
        name="fine",
    )(orbitals, pair_index.reshape(2))

    coarse_got_a = exchange(coarse_a, inner)
    coarse_got_b = exchange(coarse_b, outer)
    got = []
    got += [exchange(own[0], inner), exchange(own[1], outer)]

    whole, next_a, next_b, packed = pl.pallas_call(
        functools.partial(middle_kernel, size),
        out_shape=[shape(half + 4, mid_rows, LANES)] + [shape(3, mid_rows, LANES)] * 2 + [shape(low_rows, LANES)],
        in_specs=[VMEM] * 4,
        out_specs=[VMEM] * 4,
        scratch_shapes=[scratch(half + 4, 1, mid_tall, LANES)] * 2,
        compiler_params=params(8),
        name="middle",
    )(coarse_a, coarse_b, coarse_got_a, coarse_got_b)

    partners = list(range(0, size, 2))
    arrived = [packed]
    for k in partners[1:]:
        arrived.append(exchange(packed, [(i, i ^ k) for i in range(size) if i < i ^ k]))
    next_got_a = exchange(next_a, inner)
    next_got_b = exchange(next_b, outer)
    got += [exchange(own[2], inner), exchange(own[3], outer)]
    mine = pl.pallas_call(
        pack_kernel,
        out_shape=shape(len(partners), low_rows, LANES),
        in_specs=[VMEM] * len(partners),
        out_specs=VMEM,
        compiler_params=params(4),
        name="pack",
    )(*arrived)
    other = exchange(mine, inner)

    correction = pl.pallas_call(
        functools.partial(low_kernel, size, tuple(partners)),
        out_shape=shape(half + 4, mid_rows, LANES),
        in_specs=[ANY] * 5,
        out_specs=VMEM,
        scratch_shapes=[
            scratch(half + 10, 1, mid_tall, LANES),
            scratch(half + 8, 1, mid_tall, LANES),
            scratch(half + 6, 1, mid_tall, LANES),
            scratch(mid_rows, LANES),
            scratch(6, mid_rows, LANES),
            scratch(size + 2, low_tall, LANES),
            scratch(size + 2, low_tall, LANES),
            scratch(size + 2, low_tall, LANES),
            scratch(size + 2, low_tall, LANES),
            scratch(3, size + 2, low_rows // 2 + 2 * PAD, LANES),
            scratch(size + 2, low_rows, LANES),
            pltpu.SemaphoreType.DMA((2 * len(partners),)),
            pltpu.SemaphoreType.DMA((3,)),
        ],
        compiler_params=params(12),
        name="low",
    )(whole, next_got_a, next_got_b, mine, other)

    cells = planes * size * rows * columns
    potential, sums = pl.pallas_call(
        functools.partial(top_kernel, size, cells, cuts),
        out_shape=[shape(1, planes, rows, columns), shape(size * groups, 2, LANES)],
        in_specs=[ANY] * 8 + [VMEM, VMEM, SMEM],
        out_specs=[ANY, VMEM],
        scratch_shapes=[
            scratch(planes + 8, parts, tall, LANES),
            scratch(planes + 6, parts, tall, LANES),
            scratch(planes + 4, parts, tall, LANES),
            scratch(planes + 2, parts, tall, LANES),
            scratch(half + 4, rows, LANES),
            scratch(planes, rows, columns),
            pltpu.SemaphoreType.DMA((8,)),
            pltpu.SemaphoreType.DMA((planes,)),
        ],
        compiler_params=params(24),
        name="top",
    )(*own, *got, once, correction, pair_weight)

    everyone = lax.all_to_all(sums, ("gz", "pair"), 0, 0)
    norm, energy = pl.pallas_call(
        functools.partial(total_kernel, groups, cells),
        out_shape=[shape(1)] * 2,
        in_specs=[VMEM],
        out_specs=[SMEM] * 2,
        name="total",
    )(everyone)
    return (potential, norm, energy)


def solution(mesh):
    return jax.shard_map(
        per_device,
        mesh=mesh,
        in_specs=(P(None, "gz", None, None), P("pair", None), P("pair")),
        out_specs=(P("pair", "gz", None, None), P("pair"), P()),
        check_vma=False,
    )
```

```python
import functools

import jax
import jax.numpy as jnp
from jax import lax
from jax.experimental import pallas as pl
from jax.experimental.pallas import tpu as pltpu
from jax.sharding import PartitionSpec as P


LANES = 128
PAD = 8
SWEEPS = 8
ROWS = 32
THIRD = 1.0 / 3.0
NINTH = 1.0 / 9.0
F32 = jnp.float32
BF16 = jnp.bfloat16
ANY = pl.BlockSpec(memory_space=pl.ANY)
VMEM = pl.BlockSpec(memory_space=pltpu.VMEM)
SMEM = pl.BlockSpec(memory_space=pltpu.SMEM)
HBM = pl.BlockSpec(memory_space=pltpu.HBM)


def scale(level):
    return 4.0**level / 9.0


def iota(shape, dim):
    return lax.broadcasted_iota(jnp.int32, shape, dim)


def split_dot(value, matrix):
    high = value.astype(BF16)
    low = (value - high.astype(F32)).astype(BF16)
    return jnp.dot(high, matrix, preferred_element_type=F32) + jnp.dot(low, matrix, preferred_element_type=F32)


def to_bf16(mask, value=1.0):
    return jnp.where(mask, value, 0.0).astype(BF16)


def neighbours(ref, z, row, rows):
    parts = ref.shape[1]
    here = pl.ds(PAD + row, rows)
    centre = [ref[z, h, here, :] for h in range(parts)]
    lane = iota((rows, LANES), 1)
    after = jnp.where(lane == 0, 0.0, pltpu.roll(centre[-1], 1, 1))
    before = jnp.where(lane == LANES - 1, 0.0, pltpu.roll(centre[0], LANES - 1, 1))
    sums = []
    for h in range(parts):
        total = ref[z, h, pl.ds(PAD + row - 1, rows), :] + ref[z, h, pl.ds(PAD + row + 1, rows), :]
        total += ref[z - 1, h, here, :] + ref[z + 1, h, here, :]
        total += centre[h - 1] if h else after
        total += centre[h + 1] if h + 1 < parts else before
        sums.append(total)
    return centre, sums


def zero_pads(ref, rows):
    blank = jnp.zeros((PAD, LANES), F32)

    def plane(z, _):
        for h in range(ref.shape[1]):
            ref[z, h, pl.ds(0, PAD), :] = blank
            ref[z, h, pl.ds(PAD + rows, PAD), :] = blank
        return 0

    lax.fori_loop(0, ref.shape[0], plane, 0)


def zero_planes(ref, planes, rows):
    for z in planes:
        for h in range(ref.shape[1]):
            ref[z, h, pl.ds(PAD, rows), :] = jnp.zeros((rows, LANES), F32)


def apply_planes(dst, src, first, last, shift, rows):
    def plane(z):
        for row in range(0, rows, ROWS):
            centre, sums = neighbours(src, z, row, ROWS)
            for h in range(len(centre)):
                dst[z + shift, h, pl.ds(PAD + row, ROWS), :] = (centre[h] * 3.0 + sums[h]) * NINTH

    each_plane(first, last, plane)


def paired_rows(ref, z, rows, offset):
    return [ref[z, h, pl.ds(PAD + offset, rows // 2, stride=2), :] for h in range(ref.shape[1])]


def restrict_columns(inner, far):
    lane = iota(far.shape, 1)
    pair = [a + b for a, b in zip(inner[1], inner[2])]
    outer = far + (inner[0][0] + inner[3][0]) + (inner[0][1] + inner[3][1])
    outer += jnp.where(lane == 0, 0.0, pltpu.roll(pair[1], 1, 1))
    outer += jnp.where(lane == LANES - 1, 0.0, pltpu.roll(pair[0], LANES - 1, 1))
    return ((pair[0] + pair[1]) * 6.0 + outer) * (NINTH / 8.0)


def total_of(*lists):
    return functools.reduce(lambda a, b: a + b, [v for values in lists for v in values])


def restrict_fine(ref, z, rows):
    inner = [[a + b for a, b in zip(paired_rows(ref, z, rows, k), paired_rows(ref, z + 1, rows, k))] for k in (-1, 0, 1, 2)]
    far = total_of(*(paired_rows(ref, p, rows, k) for p in (z - 1, z + 2) for k in (0, 1)))
    return restrict_columns(inner, far)


def restrict_pair(ref, z, rows, matrices):
    half = rows // 2

    def at(plane, offset):
        return ref[plane, 0, pl.ds(PAD + offset, half, stride=2), :]

    inner = [at(z, k) + at(z + 1, k) for k in (-1, 0, 1, 2)]
    outer = inner[0] + inner[3] + (at(z - 1, 0) + at(z - 1, 1)) + (at(z + 2, 0) + at(z + 2, 1))
    total = split_dot(inner[1] + inner[2], matrices[0]) + split_dot(outer, matrices[1])
    return total * (NINTH / 8.0)


def restrict_matrices(out_shift):
    row, column = iota((LANES, LANES), 0), iota((LANES, LANES), 1) - out_shift
    inside = (column >= 0) & (column < LANES // 2)
    own = (row >> 1) == column
    beside = (row == 2 * column - 1) | (row == 2 * column + 2)
    stencil = jnp.where(inside & own, 6.0, jnp.where(inside & beside, 1.0, 0.0)).astype(BF16)
    return stencil, to_bf16(inside & own)


def deal(parts):
    n = parts * LANES
    row, column = iota((n, n), 0), iota((n, n), 1)
    return to_bf16(row == parts * (column & (LANES - 1)) + (column >> 7))


def fine_kernel(size, cuts, orbitals, pair_index, *refs):
    own, (coarse_a, coarse_b, once, left, right, source, smooth, sums, in_sem, out_sem) = refs[: 2 * len(cuts)], refs[2 * len(cuts) :]
    planes, rows = left.shape[0], left.shape[1]
    parts = source.shape[1]
    half = planes // 2
    me = lax.axis_index("gz")
    odd = me % 2

    def fetch(z):
        return [
            pltpu.make_async_copy(orbitals.at[pair_index[k], z], buffer.at[z], in_sem.at[k, z])
            for k, buffer in ((0, left), (1, right))
        ]

    for z in range(planes):
        for copy in fetch(z):
            copy.start()
    zero_pads(source, rows)
    zero_pads(smooth, rows)
    zero_planes(source, (0, planes + 1), rows)
    zero_planes(smooth, (0, 1, planes + 2, planes + 3), rows)
    dealt = deal(parts)

    def multiply(z, _):
        for copy in fetch(z):
            copy.wait()
        product = jnp.dot(left[z], dealt, preferred_element_type=F32) * jnp.dot(right[z], dealt, preferred_element_type=F32)
        for h in range(parts):
            source[z + 1, h, pl.ds(PAD, rows), :] = product[:, h * LANES : (h + 1) * LANES]
        return 0

    lax.fori_loop(0, planes, multiply, 0)

    def keep(start, target, k):
        return pltpu.make_async_copy(source.at[pl.ds(start, target.shape[0]), :, pl.ds(PAD, rows), :], target, out_sem.at[k])

    kept = []
    for k, cut in enumerate(cuts):
        kept.append(keep(1 + half * (1 - odd) + cut, own[2 * k], 2 * k))
        kept.append(keep(1 + half * odd + cut, own[2 * k + 1], 2 * k + 1))

    apply_planes(smooth, source, 1, planes + 1, 1, rows)

    def spread(target, origin):
        for h in range(parts):
            smooth[target, h, pl.ds(PAD, rows), :] = source[origin, h, pl.ds(PAD, rows), :] * NINTH

    @pl.when(me > 0)
    def _():
        spread(1, 1)

    @pl.when(me < size - 1)
    def _():
        spread(planes + 2, planes)

    for copy in kept:
        copy.start()

    kept.append(pltpu.make_async_copy(smooth.at[pl.ds(2, planes), :, pl.ds(PAD, rows), :], once, out_sem.at[2 * len(cuts)]))
    kept[-1].start()

    def coarse(q, _):
        sums[q + 1] = restrict_fine(smooth, 2 * q + 2, rows)
        return 0

    lax.fori_loop(0, half, coarse, 0)

    def edge(plane, far):
        inner = [paired_rows(smooth, plane, rows, k) for k in (-1, 0, 1, 2)]
        return restrict_columns(inner, total_of(*(paired_rows(smooth, far, rows, k) for k in (0, 1))))

    sums[0] = jnp.where(me > 0, edge(1, 2), 0.0)
    sums[half + 1] = jnp.where(me < size - 1, edge(planes + 2, planes + 1), 0.0)

    three = (half + 2) // 2

    @pl.when(odd == 0)
    def _():
        coarse_a[...] = sums[pl.ds(three, three)]
        coarse_b[...] = sums[pl.ds(0, three)]

    @pl.when(odd == 1)
    def _():
        coarse_a[...] = sums[pl.ds(0, three)]
        coarse_b[...] = sums[pl.ds(three, three)]

    for copy in kept:
        copy.wait()


def middle_kernel(size, sent_a, sent_b, got_a, got_b, whole, next_a, next_b, packed, field, smooth):
    rows = sent_a.shape[1]
    planes = whole.shape[0] - 4
    me = lax.axis_index("gz")
    zero_pads(field, rows)
    zero_pads(smooth, rows)
    first, second = restrict_matrices(0), restrict_matrices(LANES // 2)

    def gather(own, low, high):
        centre = pl.ds(PAD, rows)
        n = planes
        for plane in range(n + 4):
            value = None
            if 1 <= plane <= n + 2:
                source, at = own[(plane - 1) // ((n + 2) // 2)], (plane - 1) % ((n + 2) // 2)
                value = source[at]
            if plane < 3:
                value = low[plane] if value is None else value + low[plane]
            if plane > n:
                value = high[plane - n - 1] if value is None else value + high[plane - n - 1]
            whole[plane] = value
            field[plane, 0, centre, :] = value

    @pl.when(me % 2 == 0)
    def _():
        gather((sent_b, sent_a), got_b, got_a)

    @pl.when(me % 2 == 1)
    def _():
        gather((sent_a, sent_b), got_a, got_b)

    apply_planes(smooth, field, 1, planes + 3, 0, rows)

    @pl.when(me == 0)
    def _():
        zero_planes(smooth, (1,), rows)

    @pl.when(me == size - 1)
    def _():
        zero_planes(smooth, (planes + 2,), rows)

    packed[...] = restrict_pair(smooth, 2, rows, first) + restrict_pair(smooth, 4, rows, second)

    up, down = whole[pl.ds(1, 3)], whole[pl.ds(planes, 3)]

    @pl.when(me % 2 == 0)
    def _():
        next_a[...] = up
        next_b[...] = down

    @pl.when(me % 2 == 1)
    def _():
        next_a[...] = down
        next_b[...] = up


def packed_apply(ref, block, rows):
    centre = ref[block, pl.ds(PAD, rows), :]
    lane = iota((rows, LANES), 1)
    half = LANES // 2
    total = ref[block, pl.ds(PAD - 1, rows), :] + ref[block, pl.ds(PAD + 1, rows), :]
    other = jnp.where(lane >= half, ref[block - 1, pl.ds(PAD, rows), :], ref[block + 1, pl.ds(PAD, rows), :])
    total += pltpu.roll(centre + other, half, 1)
    total += jnp.where((lane & (half - 1)) == 0, 0.0, pltpu.roll(centre, 1, 1))
    total += jnp.where((lane & (half - 1)) == half - 1, 0.0, pltpu.roll(centre, LANES - 1, 1))
    return centre * THIRD + total * NINTH


def last_apply(ref, plane, rows, width):
    centre = ref[plane, pl.ds(PAD, rows), :]
    lane = iota((rows, LANES), 1)
    total = ref[plane, pl.ds(PAD - 1, rows), :] + ref[plane, pl.ds(PAD + 1, rows), :]
    total += ref[plane - 1, pl.ds(PAD, rows), :] + ref[plane + 1, pl.ds(PAD, rows), :]
    total += pltpu.roll(centre, 1, 1) + pltpu.roll(centre, LANES - 1, 1)
    return jnp.where(lane < width, centre * THIRD + total * NINTH, 0.0)


def coarse_levels(size, source, result, blocks, smooth, bottom, spare):
    rows = source.shape[1] - 2 * PAD
    half = rows // 2
    width = LANES // 4
    c2, c3 = scale(2), scale(3)
    row, column = iota((LANES, LANES), 0), iota((LANES, LANES), 1)
    gather = to_bf16(((row & (LANES // 2 - 1)) >> 1) == column)
    scatter = to_bf16(((column & (LANES // 2 - 1)) >> 1) == row)
    centre = pl.ds(PAD, rows)
    inner = pl.ds(PAD, half)

    for b in range(1, size + 1):
        smooth[b, centre, :] = packed_apply(source, b, rows)
    for b in range(1, size + 1):
        spare[b] = packed_apply(smooth, b, rows)
    for b in range(1, size + 1):
        pairs = spare[b, pl.ds(0, half, stride=2), :] + spare[b, pl.ds(1, half, stride=2), :]
        value = split_dot(pairs, gather) * (c3 / 8.0)
        bottom[2, b, inner, :] = value
        bottom[0, b, inner, :] = value
    now = 0
    for _ in range(SWEEPS - 1):
        for b in range(1, size + 1):
            bottom[1 - now, b, inner, :] = last_apply(bottom.at[now], b, half, width) + bottom[2, b, inner, :]
        now = 1 - now
    for b in range(1, size + 1):
        value = split_dot(bottom[now, b, inner, :], scatter)
        spare[b, pl.ds(0, half, stride=2), :] = value
        spare[b, pl.ds(1, half, stride=2), :] = value
    for b in range(1, size + 1):
        source_b = source[b, centre, :] * c2
        blocks[b, centre, :] = source_b + smooth[b, centre, :] * c2 + spare[b]
    for b in range(1, size + 1):
        smooth[b, centre, :] = packed_apply(blocks, b, rows) + source[b, centre, :] * c2
    for b in range(1, size + 1):
        result[b, centre, :] = packed_apply(smooth, b, rows) + source[b, centre, :] * c2


def each_plane(first, last, body, step=2):
    def several(k, _):
        for i in range(step):
            body(first + step * k + i)
        return 0

    lax.fori_loop(0, (last - first) // step, several, 0)
    for z in range(last - (last - first) % step, last):
        body(z)


def bring_all(pairs, sem):
    copies = [pltpu.make_async_copy(origin, target, sem.at[k]) for k, (origin, target) in enumerate(pairs)]
    for copy in copies:
        copy.start()
    return copies


def start_level(dst, src, grown, planes, shift, offset, level, rows):
    c = scale(level) * NINTH

    def plane(z):
        for r in range(0, rows, ROWS):
            centre, total = neighbours(src, z, r, ROWS)
            for h in range(len(centre)):
                value = (centre[h] * 12.0 + total[h]) * c
                dst[z + shift, h, pl.ds(PAD + r, ROWS), :] = value + grown[(z + offset) >> 1, pl.ds(r, ROWS), :]

    each_plane(*planes, plane)


def sweep_level(dst, src, source, planes, shift, offset, level, rows):
    ratio = scale(level) / NINTH

    def plane(z):
        for r in range(0, rows, ROWS):
            centre, total = neighbours(src, z, r, ROWS)
            for h in range(len(centre)):
                value = source[z + offset, h, pl.ds(PAD + r, ROWS), :]
                value = value if ratio == 1.0 else value * ratio
                dst[z + shift, h, pl.ds(PAD + r, ROWS), :] = (centre[h] * 3.0 + total[h] + value) * NINTH

    each_plane(*planes, plane)


def blank_outside(ref, me, size, halo, inside, rows):
    @pl.when(me == 0)
    def _():
        zero_planes(ref, range(halo), rows)

    @pl.when(me == size - 1)
    def _():
        zero_planes(ref, range(halo + inside, 2 * halo + inside), rows)


def pack_kernel(*refs):
    for k, ref in enumerate(refs[:-1]):
        refs[-1][k] = ref[...]


def low_kernel(size, partners, whole, next_a, next_b, mine, other, result, *scratch):
    (mid, first, second, _, grown) = scratch[:5]
    (low_source, low_result, low_blocks, low_smooth, bottom, spare, low_sem, mid_sem) = scratch[5:]
    rows = whole.shape[1]
    planes = whole.shape[0] - 4
    low_rows = mine.shape[1]
    me = lax.axis_index("gz")
    odd = me % 2
    blank = jnp.zeros((PAD, LANES), F32)
    inner = pl.ds(PAD, low_rows)
    middle = pl.ds(PAD, rows)
    edge = 3

    blocks = [
        (ref.at[k], low_source.at[jnp.bitwise_xor(me, partner ^ far) + 1, inner])
        for far, ref in ((0, mine), (1, other))
        for k, partner in enumerate(partners)
    ]
    low_copies = bring_all(blocks, low_sem)
    top = edge + planes + 4
    mid_copies = bring_all(
        [
            (whole, mid.at[pl.ds(edge, planes + 4), 0, middle]),
            (next_a, mid.at[pl.ds(top * (1 - odd), edge), 0, middle]),
            (next_b, mid.at[pl.ds(top * odd, edge), 0, middle]),
        ],
        mid_sem,
    )

    for ref in (mid, first, second):
        zero_pads(ref, rows)
    for ref in (low_source, low_blocks, low_smooth):
        for b in range(size + 2):
            ref[b, pl.ds(0, PAD), :] = blank
            ref[b, pl.ds(PAD + low_rows, PAD), :] = blank
        for b in (0, size + 1):
            ref[b, inner, :] = jnp.zeros((low_rows, LANES), F32)
    for k in range(2):
        for b in range(size + 2):
            bottom[k, b, pl.ds(0, PAD), :] = blank
            bottom[k, b, pl.ds(PAD + low_rows // 2, PAD), :] = blank
        for b in (0, size + 1):
            bottom[k, b] = jnp.zeros(bottom.shape[2:], F32)
    for b in (0, size + 1):
        low_result[b, inner, :] = jnp.zeros((low_rows, LANES), F32)
    for copy in low_copies:
        copy.wait()
    coarse_levels(size, low_source, low_result, low_blocks, low_smooth, bottom, spare)

    row, column = iota((LANES, LANES), 0), iota((LANES, LANES), 1)
    for k in range(3):
        block = low_result[me + k, inner, :]
        for side in range(2):
            value = split_dot(block, to_bf16((column >> 1) + side * (LANES // 2) == row))
            grown[2 * k + side, pl.ds(0, low_rows, stride=2), :] = value
            grown[2 * k + side, pl.ds(1, low_rows, stride=2), :] = value

    for copy in mid_copies:
        copy.wait()
    start_level(first, mid, grown, (1, planes + 9), -1, -1, 1, rows)
    blank_outside(first, me, size, 4, planes, rows)
    sweep_level(second, first, mid, (1, planes + 7), -1, 1, 1, rows)
    blank_outside(second, me, size, 3, planes, rows)
    ratio = scale(1) / NINTH

    def last(z):
        for r in range(0, rows, ROWS):
            centre, total = neighbours(second, z + 1, r, ROWS)
            value = mid[z + 3, 0, pl.ds(PAD + r, ROWS), :] * ratio
            result[z, pl.ds(r, ROWS), :] = (centre[0] * 3.0 + total[0] + value) * NINTH

    each_plane(0, planes + 4, last)


def top_kernel(size, cells, cuts, *refs):
    own, got = refs[: 2 * len(cuts)], refs[2 * len(cuts) : 4 * len(cuts)]
    once, correction, weight, third, sums, *scratch = refs[4 * len(cuts) :]
    field, first, second, grown, in_sem = scratch
    planes, parts, rows = once.shape[0], once.shape[1], once.shape[2]
    half = planes // 2
    mid_rows = correction.shape[1]
    me = lax.axis_index("gz")
    odd = me % 2

    def into(origin, plane):
        return origin, field.at[pl.ds(plane, origin.shape[0]), :, pl.ds(PAD, rows), :]

    moves = []
    for k, cut in enumerate(cuts):
        moves += [
            into(own[2 * k], half + half * (1 - odd) + cut),
            into(own[2 * k + 1], half + half * odd + cut),
            into(got[2 * k], 3 * half * (1 - odd) + cut),
            into(got[2 * k + 1], 3 * half * odd + cut),
        ]
    copies = bring_all(moves, in_sem)
    for ref in (field, first, second, third):
        zero_pads(ref, rows)

    def widen(z):
        value = correction[z]
        grown[z, pl.ds(0, mid_rows, stride=2), :] = value
        grown[z, pl.ds(1, mid_rows, stride=2), :] = value

    each_plane(0, half + 4, widen)

    for copy in copies:
        copy.wait()
    start_level(first, field, grown, (1, half), -1, 0, 0, rows)
    start_level(first, field, grown, (half + planes, 2 * half + planes - 1), -1, 0, 0, rows)
    c0 = scale(0)

    def begin(z, beside=None):
        for r in range(0, rows, ROWS):
            spread = grown[(z + half) >> 1, pl.ds(r, ROWS), :]
            for h in range(parts):
                value = field[z + half, h, pl.ds(PAD + r, ROWS), :] + once[z, h, pl.ds(r, ROWS), :]
                if beside is not None:
                    value += field[beside, h, pl.ds(PAD + r, ROWS), :] * NINTH
                first[z + 3, h, pl.ds(PAD + r, ROWS), :] = value * c0 + spread

    begin(0, half - 1)
    each_plane(1, planes - 1, begin)
    begin(planes - 1, half + planes)
    blank_outside(first, me, size, 3, planes, rows)
    sweep_level(second, first, field, (1, planes + 5), -1, 1, 0, rows)
    blank_outside(second, me, size, 2, planes, rows)
    sweep_level(third, second, field, (1, planes + 3), -1, 2, 0, rows)
    blank_outside(third, me, size, 1, planes, rows)

    def final(z, totals):
        squares, products = totals
        for r in range(0, rows, ROWS):
            centre, total = neighbours(third, z + 1, r, ROWS)
            for h in range(parts):
                f = field[z + half, h, pl.ds(PAD + r, ROWS), :]
                remain = f - 6.0 * centre[h] + total[h]
                squares += jnp.sum((remain * remain).reshape(ROWS // 8, 8, LANES), axis=0)
                products += jnp.sum((f * centre[h]).reshape(ROWS // 8, 8, LANES), axis=0)
        return squares, products

    squares, products = lax.fori_loop(0, planes // 2, lambda k, t: final(2 * k + 1, final(2 * k, t)), (jnp.zeros((8, LANES), F32),) * 2)
    products = products * (weight[0] * (-0.5 / cells))
    both = jnp.concatenate([jnp.sum(squares, axis=0, keepdims=True), jnp.sum(products, axis=0, keepdims=True)], axis=0)
    sums[...] = jnp.broadcast_to(both[None], sums.shape)


def output_kernel(third, potential, plain, sem):
    planes, parts, rows = plain.shape[0], third.shape[1], plain.shape[1]
    row, column = iota((2 * parts * LANES, parts * LANES), 0), iota((2 * parts * LANES, parts * LANES), 1)
    in_order = to_bf16(column == parts * (row & (LANES - 1)) + ((row >> 7) & (parts - 1)))

    def give(z):
        return pltpu.make_async_copy(plain.at[z], potential.at[0, z], sem.at[z])

    def plane(z):
        value = [third[z + 1, h, pl.ds(PAD, rows), :] for h in range(parts)]
        upper = [part.astype(BF16) for part in value]
        lower = [(part - high.astype(F32)).astype(BF16) for part, high in zip(value, upper)]
        plain[z] = jnp.dot(jnp.concatenate(upper + lower, axis=1), in_order, preferred_element_type=F32)
        give(z).start()

    each_plane(0, planes, plane)
    for z in range(planes):
        give(z).wait()


def total_kernel(groups, cells, everyone, norm, energy):
    values = everyone[...]
    mine = iota(values.shape, 0) % groups == lax.axis_index("pair")
    first = iota(values.shape, 1) == 0
    squares = jnp.sum(jnp.where(first & mine, values, 0.0))
    norm[0] = jnp.sqrt(jnp.full((1, 1), squares * (1.0 / cells), F32))[0, 0]
    energy[0] = jnp.sum(jnp.where(first, 0.0, values))


def exchange(value, pairs):
    return lax.ppermute(value, "gz", [move for a, b in pairs for move in ((a, b), (b, a))])


def params(mib):
    return pltpu.CompilerParams(vmem_limit_bytes=mib << 20)


def per_device(orbitals, pair_index, pair_weight):
    size = lax.axis_size("gz")
    groups = lax.axis_size("pair")
    _, planes, rows, columns = orbitals.shape
    parts = columns // LANES
    assert planes == 8 and columns == 2 * LANES and rows % (4 * ROWS) == 0 and pair_index.shape[0] == 1 and size % 2 == 0
    half = planes // 2
    mid_rows, low_rows = rows // 2, rows // 4
    tall, mid_tall, low_tall = rows + 2 * PAD, mid_rows + 2 * PAD, low_rows + 2 * PAD
    inner = [(i, i + 1) for i in range(0, size, 2)]
    outer = [(i, i + 1) for i in range(1, size - 1, 2)]

    def shape(*dims):
        return jax.ShapeDtypeStruct(dims, F32)

    def scratch(*dims):
        return pltpu.VMEM(dims, F32)

    three = (half + 2) // 2
    counts = (half // 2, half // 2)
    cuts = (0, counts[0])
    own_shapes = [shape(count, parts, rows, LANES) for count in counts for _ in range(2)]
    *own, coarse_a, coarse_b, once = pl.pallas_call(
        functools.partial(fine_kernel, size, cuts),
        out_shape=own_shapes + [shape(three, mid_rows, LANES)] * 2 + [shape(planes, parts, rows, LANES)],
        in_specs=[HBM, SMEM],
        out_specs=[ANY] * len(own_shapes) + [VMEM, VMEM, ANY],
        scratch_shapes=[
            pltpu.VMEM((planes, rows, columns), orbitals.dtype),
            pltpu.VMEM((planes, rows, columns), orbitals.dtype),
            scratch(planes + 2, parts, tall, LANES),
            scratch(planes + 4, parts, tall, LANES),
            scratch(half + 2, mid_rows, LANES),
            pltpu.SemaphoreType.DMA((2, planes)),
            pltpu.SemaphoreType.DMA((len(own_shapes) + 1,)),
        ],
        compiler_params=params(48),
        name="fine",
    )(orbitals, pair_index.reshape(2))

    coarse_got_a = exchange(coarse_a, inner)
    coarse_got_b = exchange(coarse_b, outer)
    got = []
    got += [exchange(own[0], inner), exchange(own[1], outer)]

    whole, next_a, next_b, packed = pl.pallas_call(
        functools.partial(middle_kernel, size),
        out_shape=[shape(half + 4, mid_rows, LANES)] + [shape(3, mid_rows, LANES)] * 2 + [shape(low_rows, LANES)],
        in_specs=[VMEM] * 4,
        out_specs=[VMEM] * 4,
        scratch_shapes=[scratch(half + 4, 1, mid_tall, LANES)] * 2,
        compiler_params=params(8),
        name="middle",
    )(coarse_a, coarse_b, coarse_got_a, coarse_got_b)

    partners = list(range(0, size, 2))
    arrived = [packed]
    for k in partners[1:]:
        arrived.append(exchange(packed, [(i, i ^ k) for i in range(size) if i < i ^ k]))
    next_got_a = exchange(next_a, inner)
    next_got_b = exchange(next_b, outer)
    got += [exchange(own[2], inner), exchange(own[3], outer)]
    mine = pl.pallas_call(
        pack_kernel,
        out_shape=shape(len(partners), low_rows, LANES),
        in_specs=[VMEM] * len(partners),
        out_specs=VMEM,
        compiler_params=params(4),
        name="pack",
    )(*arrived)
    other = exchange(mine, inner)

    correction = pl.pallas_call(
        functools.partial(low_kernel, size, tuple(partners)),
        out_shape=shape(half + 4, mid_rows, LANES),
        in_specs=[ANY] * 5,
        out_specs=VMEM,
        scratch_shapes=[
            scratch(half + 10, 1, mid_tall, LANES),
            scratch(half + 8, 1, mid_tall, LANES),
            scratch(half + 6, 1, mid_tall, LANES),
            scratch(mid_rows, LANES),
            scratch(6, mid_rows, LANES),
            scratch(size + 2, low_tall, LANES),
            scratch(size + 2, low_tall, LANES),
            scratch(size + 2, low_tall, LANES),
            scratch(size + 2, low_tall, LANES),
            scratch(3, size + 2, low_rows // 2 + 2 * PAD, LANES),
            scratch(size + 2, low_rows, LANES),
            pltpu.SemaphoreType.DMA((2 * len(partners),)),
            pltpu.SemaphoreType.DMA((3,)),
        ],
        compiler_params=params(12),
        name="low",
    )(whole, next_got_a, next_got_b, mine, other)

    cells = planes * size * rows * columns
    third, sums = pl.pallas_call(
        functools.partial(top_kernel, size, cells, cuts),
        out_shape=[shape(planes + 2, parts, tall, LANES), shape(size * groups, 2, LANES)],
        in_specs=[ANY] * 8 + [VMEM, VMEM, SMEM],
        out_specs=[VMEM, VMEM],
        scratch_shapes=[
            scratch(planes + 8, parts, tall, LANES),
            scratch(planes + 6, parts, tall, LANES),
            scratch(planes + 4, parts, tall, LANES),
            scratch(half + 4, rows, LANES),
            pltpu.SemaphoreType.DMA((8,)),
        ],
        compiler_params=params(24),
        name="top",
    )(*own, *got, once, correction, pair_weight)

    potential = pl.pallas_call(
        output_kernel,
        out_shape=shape(1, planes, rows, columns),
        in_specs=[VMEM],
        out_specs=ANY,
        scratch_shapes=[scratch(planes, rows, columns), pltpu.SemaphoreType.DMA((planes,))],
        compiler_params=params(8),
        cost_estimate=pl.CostEstimate(flops=10**9, bytes_accessed=10**7, transcendentals=0),
        name="output",
    )(third)
    everyone = lax.all_to_all(sums, ("gz", "pair"), 0, 0)
    norm, energy = pl.pallas_call(
        functools.partial(total_kernel, groups, cells),
        out_shape=[shape(1)] * 2,
        in_specs=[VMEM],
        out_specs=[SMEM] * 2,
        compiler_params=params(4),
        name="total",
    )(everyone)
    return (potential, norm, energy)


def solution(mesh):
    return jax.shard_map(
        per_device,
        mesh=mesh,
        in_specs=(P(None, "gz", None, None), P("pair", None), P("pair")),
        out_specs=(P("pair", "gz", None, None), P("pair"), P()),
        check_vma=False,
    )
```
